256 devices in a mesh: fsdp: 32 (over z_hi, x, y), ep: 8 (over z_lo, core).
Axes of the slice: x: 4, y: 4, z: 8 (z_hi: 2, z_lo: 4; z = z_hi * 4 + z_lo), core: 2. Of those that a mesh axis runs over, the one named last changes fastest.
Arguments:
- tokens: bfloat16 [32768, 2048], P(('fsdp', 'ep')), may hold values from -24 to 24
- routes: int32 [32768, 6], P(('fsdp', 'ep')), may hold values from 0 to 63, as said below
- route_weight: float32 [32768, 6], P(('fsdp', 'ep')), may hold values from 0.1 to 1
- w_in: bfloat16 [8, 2048, 2, 768], P('ep', 'fsdp'), may hold values from -0.125 to 0.125
- w_down: bfloat16 [8, 768, 2048], P('ep', 'fsdp'), may hold values from -0.21875 to 0.21875
- cotangent: bfloat16 [32768, 2048], P(('fsdp', 'ep')), may hold values from -6 to 6
Outputs:
- layer_out: bfloat16 [32768, 2048], P(('fsdp', 'ep'))
- grad_tokens: bfloat16 [32768, 2048], P(('fsdp', 'ep'))
- grad_in: float32 [8, 2048, 2, 768], P('ep', 'fsdp')
- grad_down: float32 [8, 768, 2048], P('ep', 'fsdp')
The draws below stay inside these ranges and needn't reach their ends.
Inputs may be any that keep to these rules, and one draw needn't show every extreme that they name: `routes`: each row names 6 different experts. The rows of one device name each window expert 0 to 7 at most 32 times; in every draw every device names some window expert exactly 32 times, and for some index of fsdp one window expert is named exactly 32 times by each device with that index.
All inputs are finite; a program needn't handle non-finite values.
Results may differ from the reference program's by a relative error of at most 0.014.
Values may be sent and summed in bfloat16 or wider, within the bound.
A program may use at most 64 MiB of HBM per device.

```python
import jax
import jax.numpy as jnp
from jax import lax

D = 2048
FF = 768
EXPERTS = 64
TOP = 6
TOK_DEV = 128
CAP = 32
WIN = 8
TOKENS = 32768
N_EP = 8


def draw_routes(key, part):
    blocks = TOKENS // TOK_DEV
    spacing = TOK_DEV // WIN
    key_order = jax.random.fold_in(key, 11)
    key_count = jax.random.fold_in(key, 12)
    key_full = jax.random.fold_in(key, 13)
    key_group = jax.random.fold_in(key, 14)
    key_expert = jax.random.fold_in(key, 15)
    key_rank = jax.random.fold_in(key, 16)
    key_shuffle = jax.random.fold_in(key, 17)
    token_order = jax.vmap(lambda one_key: jax.random.permutation(one_key, TOK_DEV))(jax.random.split(key_order, blocks))
    counts = jax.random.randint(key_count, (blocks, WIN), 1, CAP + 1)
    window_ids = jnp.arange(WIN, dtype=jnp.int32)
    full_pick = jax.random.randint(key_full, (blocks, 1), 0, WIN)
    counts = jnp.where(window_ids[None, :] == full_pick, CAP, counts)
    group_pick = jax.random.randint(key_group, (), 0, blocks // WIN)
    expert_pick = jax.random.randint(key_expert, (), 0, WIN)
    block_group = jnp.arange(blocks, dtype=jnp.int32) // WIN
    chosen_cells = (block_group[:, None] == group_pick) & (window_ids[None, :] == expert_pick)
    counts = jnp.where(chosen_cells, CAP, counts)
    offsets = (token_order[:, :, None] - spacing * window_ids[None, None, :]) % TOK_DEV
    member = (offsets < counts[:, None, :]).reshape(TOKENS, WIN)
    expert_ids = jnp.arange(EXPERTS, dtype=jnp.int32)
    ranks = jax.vmap(lambda one_key: jax.random.permutation(one_key, EXPERTS))(jax.random.split(key_rank, TOKENS)).astype(jnp.int32)
    member_full = jnp.concatenate([member, jnp.zeros((TOKENS, EXPERTS - WIN), jnp.bool_)], axis=1)
    scores = jnp.where(expert_ids[None, :] < WIN, jnp.where(member_full, EXPERTS + ranks, -1 - expert_ids[None, :]), ranks)
    chosen = lax.top_k(scores, TOP)[1].astype(jnp.int32)
    shuffle = jax.vmap(lambda one_key: jax.random.permutation(one_key, TOP))(jax.random.split(key_shuffle, TOKENS))
    return jnp.take_along_axis(chosen, shuffle.astype(jnp.int32), axis=1).astype(jnp.int32)


def strengthened(result, own_key, source, target, shards_of, factor):
    owner, partner = [(jnp.arange(result.shape[axis_at]) // (result.shape[axis_at] // shards_of)).reshape([-1 if axis == axis_at else 1 for axis in range(result.ndim)]) for axis_at in (source, target)]
    chosen = jax.random.permutation(own_key, shards_of)[partner]
    strong = (owner == chosen) | (owner == (partner + shards_of // 2) % shards_of)
    return jnp.where(strong, factor * result, result)


def block_scale(stream_key, dims, cuts, least, high):
    def one(dim, shards_of):
        steps = jax.random.uniform(jax.random.fold_in(jax.random.fold_in(stream_key, 6), dim), (shards_of,), jnp.float32, least / len(cuts), high / len(cuts))
        return jnp.repeat(jnp.exp(steps), dims[dim] // shards_of).reshape((-1,) + (1,) * (len(dims) - dim - 1))

    factor_of = one(*cuts[0])
    for cut in cuts[1:]:
        factor_of = factor_of * one(*cut)
    return factor_of


def bell_draw(rng, dims, spread, reach, pieces=(), kind=jnp.bfloat16):
    values = jax.random.normal(rng, dims, jnp.float32) * spread
    if len(pieces) > 0:
        values = block_scale(rng, dims, pieces, -0.22, 0.18) * values
    return jnp.clip(values, min=-reach, max=reach).astype(kind)


def heavy_noise(stream_key, dims, width, reach, pieces, heavy, kind=jnp.bfloat16):
    entries = width * jax.random.normal(stream_key, dims, jnp.float32)
    if pieces:
        entries = entries * block_scale(stream_key, dims, pieces, -0.22, 0.18)
    return jnp.clip(strengthened(entries, jax.random.fold_in(stream_key, 3), *heavy), -reach, reach).astype(kind)


def setup_inputs(seed: int = 0) -> dict:
    arg_keys = jax.random.split(jax.random.key(seed), 7)
    tokens = heavy_noise(arg_keys[0], (TOKENS, D), 1.0, 24.0, ((0, 256),), (0, 1, 256, 6.0))
    routes = draw_routes(jax.random.fold_in(arg_keys[6], 71), 0)
    route_weight = jnp.clip(0.1 + 0.9 * jax.random.uniform(arg_keys[2], (TOKENS, TOP), jnp.float32) ** block_scale(arg_keys[2], (TOKENS, TOP), ((0, 256),), -0.2, 0.2), 0.1, 1.0)
    w_in = bell_draw(arg_keys[3], (WIN, D, 2, FF), D ** -0.5, 0.125, ((0, 8), (1, 32)))
    w_down = bell_draw(arg_keys[4], (WIN, FF, D), FF ** -0.5, 0.21875, ((0, 8), (1, 32)))
    cotangent = bell_draw(arg_keys[5], (TOKENS, D), 1.0, 6.0, ((0, 256),))
    return {"tokens": tokens, "routes": routes, "route_weight": route_weight, "w_in": w_in, "w_down": w_down, "cotangent": cotangent}


def reference(tokens, routes, route_weight, w_in, w_down, cotangent):
    group = N_EP * TOK_DEV
    rows_cap = N_EP * CAP
    groups = TOKENS // group

    def one_group(carry, inputs):
        sum_in, sum_down = carry
        group_tokens, group_routes, group_weights, group_grads = inputs
        mixed_rows = jnp.zeros((group, D), jnp.float32)
        input_grads = jnp.zeros((group, D), jnp.float32)
        part_in = []
        part_down = []
        for expert in range(N_EP):
            route_hits = group_routes == expert
            member = jnp.any(route_hits, axis=1)
            route_coef = jnp.sum(jnp.where(route_hits, group_weights, jnp.zeros_like(group_weights)), axis=1)
            member_int = member.astype(jnp.int32)
            slot_rank = (jnp.cumsum(member_int) - member_int).astype(jnp.int32)
            target = jnp.where(member, slot_rank, rows_cap).astype(jnp.int32)
            row_index = jnp.zeros((rows_cap,), jnp.int32).at[target].set(jnp.arange(group, dtype=jnp.int32), mode="drop")
            is_valid = jnp.zeros((rows_cap,), jnp.float32).at[target].set(1.0, mode="drop")
            rows_x = group_tokens[row_index] * is_valid[:, None].astype(group_tokens.dtype)
            flat_in = w_in[expert].reshape(D, 2 * FF)
            gate_up = jnp.dot(rows_x, flat_in, preferred_element_type=jnp.float32)
            gate_vals = gate_up[:, :FF]
            up_vals = gate_up[:, FF:]
            sig_gate = jax.nn.sigmoid(gate_vals)
            act_vals = gate_vals * sig_gate
            hidden = (act_vals * up_vals).astype(jnp.bfloat16)
            out_rows = jnp.dot(hidden, w_down[expert], preferred_element_type=jnp.float32).astype(jnp.bfloat16)
            row_coef = route_coef[row_index] * is_valid
            mixed_rows = mixed_rows.at[row_index].add(row_coef[:, None] * out_rows.astype(jnp.float32))
            grad_rows = (row_coef[:, None] * group_grads[row_index].astype(jnp.float32)).astype(jnp.bfloat16)
            grad_hidden = jnp.dot(grad_rows, w_down[expert].T, preferred_element_type=jnp.float32)
            grad_gate = grad_hidden * up_vals * sig_gate * (1.0 + gate_vals * (1.0 - sig_gate))
            grad_up = grad_hidden * act_vals
            grad_gu = jnp.concatenate([grad_gate, grad_up], axis=1).astype(jnp.bfloat16)
            input_rows = jnp.dot(grad_gu, flat_in.T, preferred_element_type=jnp.float32).astype(jnp.bfloat16)
            input_grads = input_grads.at[row_index].add(input_rows.astype(jnp.float32) * is_valid[:, None])
            term_in = lax.optimization_barrier(jnp.dot(rows_x.T, grad_gu, preferred_element_type=jnp.float32).astype(jnp.bfloat16))
            term_down = lax.optimization_barrier(jnp.dot(hidden.T, grad_rows, preferred_element_type=jnp.float32).astype(jnp.bfloat16))
            part_in.append(term_in.astype(jnp.float32))
            part_down.append(term_down.astype(jnp.float32))
        sum_in = sum_in + jnp.stack(part_in)
        sum_down = sum_down + jnp.stack(part_down)
        return (sum_in, sum_down), (mixed_rows, input_grads)

    init = (jnp.zeros((N_EP, D, 2 * FF), jnp.float32), jnp.zeros((N_EP, FF, D), jnp.float32))
    inputs = (tokens.reshape(groups, group, D), routes.reshape(groups, group, TOP),
              route_weight.reshape(groups, group, TOP), cotangent.reshape(groups, group, D))
    (sum_in, sum_down), (mixed_all, grads_all) = lax.scan(one_group, init, inputs)
    layer_out = mixed_all.reshape(TOKENS, D).astype(jnp.bfloat16)
    grad_tokens = grads_all.reshape(TOKENS, D).astype(jnp.bfloat16)
    return layer_out, grad_tokens, sum_in.reshape(N_EP, D, 2, FF), sum_down
```

```python
import jax
import jax.numpy as jnp
from jax import lax
from jax.experimental import pallas as pl
from jax.experimental.pallas import tpu as pltpu
from jax.sharding import PartitionSpec as P

D = 2048
FF = 768
CAP = 32
MESH = pl.DeviceIdType.MESH
F32 = jnp.float32
BF16 = jnp.bfloat16
N_SEM_A = 200
N_SEM_B = 220


def rem(value, modulus):
    return lax.rem(value, jnp.int32(modulus))


def div(value, divisor):
    return lax.div(value, jnp.int32(divisor))


def place():
    f = lax.axis_index("fsdp")
    e = lax.axis_index("ep")
    return rem(div(f, 4), 4), rem(f, 4), div(f, 16) * 4 + div(e, 2), rem(e, 2)


def device(x, y, z, c):
    return (div(z, 4) * 16 + x * 4 + y, rem(z, 4) * 2 + c)


def greet(x, y, z, c):
    barrier = pltpu.get_barrier_semaphore()
    peers = [device(rem(x + o, 4), y, z, c) for o in (1, 3)]
    peers += [device(x, rem(y + o, 4), z, c) for o in (1, 3)]
    peers += [device(x, y, rem(z + 4, 8), c), device(x, y, z, 1 - c)]
    peers += [device(x, y, rem(z + o, 8), k) for o in (1, 7, 2, 6) for k in (0, 1)]
    for peer in peers:
        pl.semaphore_signal(barrier, inc=1, device_id=peer, device_id_type=MESH)
    pl.semaphore_wait(barrier, len(peers))


class Link:
    def __init__(self, send_sem, recv_sem, limit):
        self.send_sem, self.recv_sem, self.limit = send_sem, recv_sem, limit
        self.number, self.sent = {}, []

    def index(self, key):
        number = self.number.setdefault(key, len(self.number))
        assert number < self.limit
        return number

    def send(self, key, src, dst, to):
        k = self.index(key)
        copy = pltpu.make_async_remote_copy(
            src_ref=src, dst_ref=dst, send_sem=self.send_sem.at[k], recv_sem=self.recv_sem.at[k],
            device_id=to, device_id_type=MESH,
        )
        copy.start()
        self.sent.append(copy)

    def wait(self, key, dst):
        k = self.index(key)
        pltpu.make_async_remote_copy(
            src_ref=dst, dst_ref=dst, send_sem=self.send_sem.at[k], recv_sem=self.recv_sem.at[k],
            device_id=place_id(), device_id_type=MESH,
        ).wait_recv()

    def drain(self):
        for copy in self.sent:
            copy.wait_send()


def place_id():
    return (lax.axis_index("fsdp"), lax.axis_index("ep"))


def part(kind, ref, p=None, h=None):
    if p is None:
        return ref
    size = (32 if kind == "in" else 1024) // (1 if h is None else 2)
    start = (32 if kind == "in" else 1024) * p + size * (h or 0)
    if kind == "in":
        return ref.at[pl.ds(start, size), :]
    return ref.at[:, pl.ds(start, size)]


def exchange_targets(x, y, z, c):
    out = []
    for kind, off in ((0, 0), (1, 1), (2, 7), (3, 2 + 4 * c)):
        for k in (0, 1):
            out.append((kind, k, rem(z + off, 8)))
    return out


def gather_kernel(win, wdn, sx, sdy, fin, fdn, rx, rdy, send_sem, recv_sem, a_send, a_recv, local_sem):
    x, y, z, c = place()
    zh = div(z, 4)
    greet(x, y, z, c)
    link = Link(send_sem, recv_sem, N_SEM_A)
    full = {"in": fin, "dn": fdn}
    own = {"in": win, "dn": wdn}
    kinds = ("dn", "in")
    zs = (zh, 1 - zh)
    to_x = {s: device(rem(x + s, 4), y, z, c) for s in (1, 3)}
    to_y = {s: device(x, rem(y + s, 4), z, c) for s in (1, 3)}

    def slot(kind, q, xo, yo, p=None, h=None):
        return part(kind, full[kind].at[zs[q], rem(x + xo, 4), rem(y + yo, 4)], p, h)

    for n, kind in enumerate(kinds):
        link.send(("z", kind), own[kind], slot(kind, 0, 0, 0), device(x, y, rem(z + 4, 8), c))

    def start(q):
        for kind in kinds:
            src = own[kind] if q == 0 else slot(kind, q, 0, 0)
            for s in (1, 3):
                link.send(("x0", q, kind, s), src, slot(kind, q, 0, 0), to_x[s])
                link.send(("y0", q, kind, s), src, slot(kind, q, 0, 0), to_y[s])

    def first(q):
        for kind in kinds:
            for s in (1, 3):
                h = 0 if s == 1 else 1
                link.wait(("x0", q, kind, s), slot(kind, q, 4 - s, 0))
                for p in (0, 1):
                    piece = slot(kind, q, 4 - s, 0, p, h)
                    link.send(("xf", q, kind, p, 0, s), piece, piece, to_x[s])
                for t in (1, 3):
                    piece = slot(kind, q, 4 - s, 0, 0)
                    link.send(("y2", q, kind, 4 - s, t), piece, piece, to_y[t])
                link.wait(("y0", q, kind, s), slot(kind, q, 0, 4 - s))
                for p in (0, 1):
                    piece = slot(kind, q, 0, 4 - s, p, h)
                    link.send(("yf", q, kind, p, 0, s), piece, piece, to_y[s])
                for t in (1, 3):
                    piece = slot(kind, q, 0, 4 - s, 1)
                    link.send(("x2", q, kind, 4 - s, t), piece, piece, to_x[t])

    def second(q):
        for kind in kinds:
            for s in (1, 3):
                h = 0 if s == 1 else 1
                link.wait(("xf", q, kind, 0, 0, s), slot(kind, q, 2, 0, 0, h))
                link.wait(("yf", q, kind, 1, 0, s), slot(kind, q, 0, 2, 1, h))
            for t in (1, 3):
                piece = slot(kind, q, 2, 0, 0)
                link.send(("y2", q, kind, 2, t), piece, piece, to_y[t])
                piece = slot(kind, q, 0, 2, 1)
                link.send(("x2", q, kind, 2, t), piece, piece, to_x[t])

    def third(q, offsets):
        for kind in kinds:
            for o in offsets:
                for s in (1, 3):
                    h = 0 if s == 1 else 1
                    link.wait(("y2", q, kind, o, s), slot(kind, q, o, 4 - s, 0))
                    piece = slot(kind, q, o, 4 - s, 0, h)
                    link.send(("yf", q, kind, 0, o, s), piece, piece, to_y[s])
                    link.wait(("x2", q, kind, o, s), slot(kind, q, 4 - s, o, 1))
                    piece = slot(kind, q, 4 - s, o, 1, h)
                    link.send(("xf", q, kind, 1, o, s), piece, piece, to_x[s])

    def last(q):
        for kind in kinds:
            for s in (1, 3):
                h = 0 if s == 1 else 1
                for o in range(4):
                    link.wait(("yf", q, kind, 0, o, s), slot(kind, q, o, 2, 0, h))
                    link.wait(("xf", q, kind, 1, o, s), slot(kind, q, 2, o, 1, h))

    start(0)
    locals_ = []
    for n, kind in enumerate(kinds):
        locals_.append(pltpu.make_async_copy(own[kind], slot(kind, 0, 0, 0), local_sem.at[n]))
    mine = rem(z, 4) * 2 + c
    locals_.append(pltpu.make_async_copy(sx.at[mine], rx.at[c], local_sem.at[2]))
    locals_.append(pltpu.make_async_copy(sdy.at[mine], rdy.at[c], local_sem.at[3]))
    for copy in locals_:
        copy.start()
    first(0)
    for kind in kinds:
        link.wait(("z", kind), slot(kind, 1, 0, 0))
    start(1)
    rows = []
    for which, (src, dst) in enumerate(((sx, rx), (sdy, rdy))):
        for kind, k, zd in exchange_targets(x, y, z, c):
            if kind == 0:
                if k:
                    continue
                core = 1 - c
            else:
                core = k
            expert = rem(zd, 4) * 2 + core
            number = which * 8 + 2 * kind + c
            copy = pltpu.make_async_remote_copy(
                src_ref=src.at[expert], dst_ref=dst.at[2 * kind + c], send_sem=a_send.at[which * 8 + 2 * kind + k],
                recv_sem=a_recv.at[number], device_id=device(x, y, zd, core), device_id_type=MESH,
            )
            copy.start()
            rows.append(copy)
    second(0)
    third(0, (1, 3))
    first(1)
    third(0, (2,))
    second(1)
    third(1, (1, 3))
    third(1, (2,))
    last(0)
    last(1)
    for which, dst in enumerate((rx, rdy)):
        for number in range(1, 8):
            s = number if number > 1 else 1 - c
            pltpu.make_async_remote_copy(
                src_ref=dst.at[s], dst_ref=dst.at[s], send_sem=a_send.at[which * 8 + number],
                recv_sem=a_recv.at[which * 8 + s], device_id=place_id(), device_id_type=MESH,
            ).wait_recv()
    for copy in locals_:
        copy.wait()
    for copy in rows:
        copy.wait_send()
    link.drain()


def gather(win, wdn, sx, sdy):
    anyspace = pl.BlockSpec(memory_space=pl.ANY)
    return pl.pallas_call(
        gather_kernel,
        name="weights_and_rows_in",
        out_shape=(
            jax.ShapeDtypeStruct((2, 4, 4, 64, 2 * FF), BF16),
            jax.ShapeDtypeStruct((2, 4, 4, 24, D), BF16),
            jax.ShapeDtypeStruct((8, CAP, D), BF16),
            jax.ShapeDtypeStruct((8, CAP, D), BF16),
        ),
        in_specs=[anyspace] * 4,
        out_specs=[anyspace] * 4,
        scratch_shapes=[
            pltpu.SemaphoreType.DMA((N_SEM_A,)),
            pltpu.SemaphoreType.DMA((N_SEM_A,)),
            pltpu.SemaphoreType.DMA((16,)),
            pltpu.SemaphoreType.DMA((16,)),
            pltpu.SemaphoreType.DMA((4,)),
        ],
        compiler_params=pltpu.CompilerParams(collective_id=0, has_side_effects=True),
    )(win, wdn, sx, sdy)


def scatter_kernel(tin_hbm, tdn_hbm, ox, odx, gin, gdn, box, bdx,
                   tin, tdn, a_in, a_dn, b_in, b_dn, c_in, c_dn, d_in, d_dn, e_in, e_dn,
                   send_sem, recv_sem, r_send, r_recv, local_sem):
    x, y, z, c = place()
    zh = div(z, 4)
    e = lax.axis_index("ep")
    link = Link(send_sem, recv_sem, N_SEM_B)
    term = {"in": tin, "dn": tdn}
    buf_a = {"in": a_in, "dn": a_dn}
    buf_b = {"in": b_in, "dn": b_dn}
    buf_c = {"in": c_in, "dn": c_dn}
    buf_d = {"in": d_in, "dn": d_dn}
    buf_e = {"in": e_in, "dn": e_dn}
    kinds = ("dn", "in")
    zs = (1 - zh, zh)
    loads = []
    for q in (0, 1):
        for n, (src, dst) in enumerate(((tdn_hbm, tdn), (tin_hbm, tin))):
            copy = pltpu.make_async_copy(src.at[zs[q]], dst.at[zs[q]], local_sem.at[2 * q + n])
            copy.start()
            loads.append(copy)
    own_rows = []
    for which, (src, dst) in enumerate(((ox, box), (odx, bdx))):
        copy = pltpu.make_async_copy(src.at[c], dst.at[e], local_sem.at[4 + which])
        copy.start()
        own_rows.append(copy)
    greet(x, y, z, c)
    to = {0: {s: device(x, rem(y + s, 4), z, c) for s in (1, 3)},
          1: {s: device(rem(x + s, 4), y, z, c) for s in (1, 3)}}

    def slot(kind, q, p, first, other, h=None):
        xo, yo = (other, first) if p == 0 else (first, other)
        return part(kind, term[kind].at[zs[q], rem(x + xo, 4), rem(y + yo, 4)], p, h)

    def add(dst, *srcs):
        total = dst[...].astype(F32)
        for src in srcs:
            total = total + src[...].astype(F32)
        dst[...] = total.astype(BF16)

    offsets = (2, 1, 3, 0)

    def r1(q):
        for o in offsets:
            for kind in kinds:
                for p in (0, 1):
                    for s, h in ((3, 0), (1, 1)):
                        link.send(("a", q, kind, p, o, s), slot(kind, q, p, 2, o, h),
                                  buf_a[kind].at[p, q, o, h], to[p][s])

    def r2(q):
        for o in offsets:
            for kind in kinds:
                for p in (0, 1):
                    for s, h in ((3, 0), (1, 1)):
                        link.wait(("a", q, kind, p, o, s), buf_a[kind].at[p, q, o, h])
                        add(slot(kind, q, p, s, o, h), buf_a[kind].at[p, q, o, h])
                        link.send(("b", q, kind, p, o, s), slot(kind, q, p, s, o),
                                  buf_b[kind].at[p, q, o, h], to[p][s])

    def r3(q):
        for o in offsets:
            for kind in kinds:
                for p in (0, 1):
                    for s, h in ((3, 0), (1, 1)):
                        link.wait(("b", q, kind, p, o, s), buf_b[kind].at[p, q, o, h])
                    add(slot(kind, q, p, 0, o), buf_b[kind].at[p, q, o, 0], buf_b[kind].at[p, q, o, 1])
                    if o == 2:
                        for s, h in ((3, 0), (1, 1)):
                            link.send(("c", q, kind, p, s), slot(kind, q, p, 0, 2, h),
                                      buf_c[kind].at[p, q, h], to[1 - p][s])
        for s, h in ((3, 0), (1, 1)):
            for kind in kinds:
                for p in (0, 1):
                    link.wait(("c", q, kind, p, s), buf_c[kind].at[p, q, h])
                    add(slot(kind, q, p, 0, s, h), buf_c[kind].at[p, q, h])
                    link.send(("d", q, kind, p, s), slot(kind, q, p, 0, s), buf_d[kind].at[p, q, h], to[1 - p][s])

    def wait_d(q):
        for kind in kinds:
            for p in (0, 1):
                for s, h in ((3, 0), (1, 1)):
                    link.wait(("d", q, kind, p, s), buf_d[kind].at[p, q, h])

    partner = device(x, y, rem(z + 4, 8), c)

    def r4(q):
        wait_d(q)
        for kind in kinds:
            for p in (0, 1):
                add(slot(kind, q, p, 0, 0), buf_d[kind].at[p, q, 0], buf_d[kind].at[p, q, 1])
            link.send(("e", kind), term[kind].at[zs[0], x, y], buf_e[kind], partner)

    loads[0].wait()
    loads[1].wait()
    r1(0)
    rows = []
    for which, (src, dst) in enumerate(((ox, box), (odx, bdx))):
        for number in range(1, 8):
            if number == 1:
                s, zd, core = 1 - c, z, 1 - c
            else:
                off = {2: 7, 3: 7, 4: 1, 5: 1, 6: 6, 7: 2}[number]
                s, zd, core = number, rem(z + off, 8), number % 2
            key = 2 * (number // 2) + c
            copy = pltpu.make_async_remote_copy(
                src_ref=src.at[s], dst_ref=dst.at[e], send_sem=r_send.at[which * 8 + number],
                recv_sem=r_recv.at[which * 8 + key], device_id=device(x, y, zd, core), device_id_type=MESH,
            )
            copy.start()
            rows.append(copy)
    loads[2].wait()
    loads[3].wait()
    r1(1)
    r2(0)
    r2(1)
    r3(0)
    r4(0)
    r3(1)
    wait_d(1)
    for kind in kinds:
        link.wait(("e", kind), buf_e[kind])
    for kind, out in (("dn", gdn), ("in", gin)):
        for p in (0, 1):
            total = slot(kind, 1, p, 0, 0)[...].astype(F32) + buf_d[kind][p, 1, 0].astype(F32)
            total = total + buf_d[kind][p, 1, 1].astype(F32)
            total = total + part(kind, buf_e[kind], p)[...].astype(F32)
            part(kind, out, p)[...] = total
    for which, dst in enumerate((box, bdx)):
        for kind, k, zd in exchange_targets(x, y, z, c):
            if kind == 0:
                if k:
                    continue
                core = 1 - c
            else:
                core = k
            expert = rem(zd, 4) * 2 + core
            number = which * 8 + 2 * kind + core
            pltpu.make_async_remote_copy(
                src_ref=dst.at[expert], dst_ref=dst.at[expert], send_sem=r_send.at[which * 8 + 1],
                recv_sem=r_recv.at[number], device_id=place_id(), device_id_type=MESH,
            ).wait_recv()
    for copy in own_rows:
        copy.wait()
    for copy in rows:
        copy.wait_send()
    link.drain()


def scatter(tin, tdn, out_rows, dx_rows):
    anyspace = pl.BlockSpec(memory_space=pl.ANY)
    vmem = pl.BlockSpec(memory_space=pltpu.VMEM)
    return pl.pallas_call(
        scatter_kernel,
        name="gradients_and_rows_out",
        out_shape=(
            jax.ShapeDtypeStruct((64, 2 * FF), F32),
            jax.ShapeDtypeStruct((24, D), F32),
            jax.ShapeDtypeStruct((8, CAP, D), BF16),
            jax.ShapeDtypeStruct((8, CAP, D), BF16),
        ),
        in_specs=[anyspace] * 4,
        out_specs=[vmem, vmem, anyspace, anyspace],
        scratch_shapes=[
            pltpu.VMEM((2, 4, 4, 64, 2 * FF), BF16),
            pltpu.VMEM((2, 4, 4, 24, D), BF16),
            pltpu.VMEM((2, 2, 4, 2, 16, 2 * FF), BF16),
            pltpu.VMEM((2, 2, 4, 2, 24, 512), BF16),
            pltpu.VMEM((2, 2, 4, 2, 32, 2 * FF), BF16),
            pltpu.VMEM((2, 2, 4, 2, 24, 1024), BF16),
            pltpu.VMEM((2, 2, 2, 16, 2 * FF), BF16),
            pltpu.VMEM((2, 2, 2, 24, 512), BF16),
            pltpu.VMEM((2, 2, 2, 32, 2 * FF), BF16),
            pltpu.VMEM((2, 2, 2, 24, 1024), BF16),
            pltpu.VMEM((64, 2 * FF), BF16),
            pltpu.VMEM((24, D), BF16),
            pltpu.SemaphoreType.DMA((N_SEM_B,)),
            pltpu.SemaphoreType.DMA((N_SEM_B,)),
            pltpu.SemaphoreType.DMA((16,)),
            pltpu.SemaphoreType.DMA((16,)),
            pltpu.SemaphoreType.DMA((6,)),
        ],
        compiler_params=pltpu.CompilerParams(
            collective_id=1, has_side_effects=True, vmem_limit_bytes=48 * 1024 * 1024
        ),
    )(tin, tdn, out_rows, dx_rows)


def contract_rows(left, right):
    return lax.dot_general(left, right, (((0,), (0,)), ((), ())), preferred_element_type=F32)


def contract_cols(left, right):
    return lax.dot_general(left, right, (((1,), (1,)), ((), ())), preferred_element_type=F32)


def local(tokens, routes, route_weight, w_in, w_down, cotangent):
    ep_width = lax.axis_size("ep")
    all_rows = ep_width * CAP
    expert_ids = jnp.arange(ep_width, dtype=jnp.int32)
    route_hits = routes[:, :, None] == expert_ids[None, None, :]
    member = jnp.any(route_hits, axis=1).astype(jnp.int32)
    route_coef = jnp.sum(jnp.where(route_hits, route_weight[:, :, None], 0.0), axis=1)
    slot_rank = jnp.cumsum(member, axis=0) - member
    slot_ids = jnp.arange(CAP, dtype=jnp.int32)
    slot_hits = (slot_rank.T[:, None, :] == slot_ids[None, :, None]) & (member.T[:, None, :] > 0)
    dispatch = slot_hits.astype(BF16)
    slot_coef = jnp.sum(jnp.where(slot_hits, route_coef.T[:, None, :], 0.0), axis=2)
    weighted_dispatch = jnp.where(slot_hits, route_coef.T[:, None, :], 0.0)
    send_x = jnp.einsum("est,td->esd", dispatch, tokens, preferred_element_type=F32).astype(BF16)
    dy_rows = jnp.einsum("est,td->esd", dispatch, cotangent, preferred_element_type=F32)
    send_dy = (dy_rows * slot_coef[:, :, None]).astype(BF16)

    full_in, full_down, recv_x, recv_dy = gather(w_in[0].reshape(64, 2 * FF), w_down[0], send_x, send_dy)
    flat_in = full_in.reshape(D, 2 * FF)
    full_down = full_down.reshape(FF, D)
    rows_x = recv_x.reshape(all_rows, D)
    rows_dy = recv_dy.reshape(all_rows, D)
    gate_up = jnp.dot(rows_x, flat_in, preferred_element_type=F32)
    gate_vals = gate_up[:, :FF]
    up_vals = gate_up[:, FF:]
    sig_gate = jax.nn.sigmoid(gate_vals)
    act_vals = gate_vals * sig_gate
    hidden = (act_vals * up_vals).astype(BF16)
    out_rows = jnp.dot(hidden, full_down, preferred_element_type=F32).astype(BF16)
    grad_hidden = contract_cols(rows_dy, full_down)
    grad_gate = grad_hidden * up_vals * sig_gate * (1.0 + gate_vals * (1.0 - sig_gate))
    grad_up = grad_hidden * act_vals
    grad_gu = jnp.concatenate([grad_gate, grad_up], axis=1).astype(BF16)
    input_rows = contract_cols(grad_gu, flat_in).astype(BF16)
    term_in = contract_rows(rows_x, grad_gu).astype(BF16)
    term_down = contract_rows(hidden, rows_dy).astype(BF16)
    grad_in, grad_down, back_out, back_dx = scatter(
        term_in.reshape(2, 4, 4, 64, 2 * FF), term_down.reshape(2, 4, 4, 24, D),
        out_rows.reshape(ep_width, CAP, D), input_rows.reshape(ep_width, CAP, D),
    )
    mixed_sum = jnp.einsum("est,esd->td", weighted_dispatch, back_out.astype(F32), preferred_element_type=F32)
    grad_sum = jnp.einsum("est,esd->td", dispatch, back_dx, preferred_element_type=F32)
    return (
        mixed_sum.astype(BF16),
        grad_sum.astype(BF16),
        grad_in.reshape(w_in.shape),
        grad_down.reshape(w_down.shape),
    )


def solution(mesh):
    in_specs = (
        P(("fsdp", "ep"), None),
        P(("fsdp", "ep"), None),
        P(("fsdp", "ep"), None),
        P("ep", "fsdp", None, None),
        P("ep", "fsdp", None),
        P(("fsdp", "ep"), None),
    )
    out_specs = (
        P(("fsdp", "ep"), None),
        P(("fsdp", "ep"), None),
        P("ep", "fsdp", None, None),
        P("ep", "fsdp", None),
    )
    return jax.shard_map(local, mesh=mesh, in_specs=in_specs, out_specs=out_specs, check_vma=False)
```

```python
import jax
import jax.numpy as jnp
from jax import lax
from jax.experimental import pallas as pl
from jax.experimental.pallas import tpu as pltpu
from jax.sharding import PartitionSpec as P

D = 2048
FF = 768
CAP = 32
MESH = pl.DeviceIdType.MESH
F32 = jnp.float32
BF16 = jnp.bfloat16
N_SEM_A = 200
N_SEM_B = 220
ROWS = 8 * CAP


def rem(value, modulus):
    return lax.rem(value, jnp.int32(modulus))


def div(value, divisor):
    return lax.div(value, jnp.int32(divisor))


def place():
    f = lax.axis_index("fsdp")
    e = lax.axis_index("ep")
    return rem(div(f, 4), 4), rem(f, 4), div(f, 16) * 4 + div(e, 2), rem(e, 2)


def device(x, y, z, c):
    return (div(z, 4) * 16 + x * 4 + y, rem(z, 4) * 2 + c)


def greet(x, y, z, c):
    barrier = pltpu.get_barrier_semaphore()
    peers = [device(rem(x + o, 4), y, z, c) for o in (1, 3)]
    peers += [device(x, rem(y + o, 4), z, c) for o in (1, 3)]
    peers += [device(x, y, rem(z + 4, 8), c), device(x, y, z, 1 - c)]
    peers += [device(x, y, rem(z + o, 8), k) for o in (1, 7, 2, 6) for k in (0, 1)]
    for peer in peers:
        pl.semaphore_signal(barrier, inc=1, device_id=peer, device_id_type=MESH)
    pl.semaphore_wait(barrier, len(peers))


class Link:
    def __init__(self, send_sem, recv_sem, limit):
        self.send_sem, self.recv_sem, self.limit = send_sem, recv_sem, limit
        self.number, self.sent = {}, []

    def index(self, key):
        number = self.number.setdefault(key, len(self.number))
        assert number < self.limit
        return number

    def send(self, key, src, dst, to):
        k = self.index(key)
        copy = pltpu.make_async_remote_copy(
            src_ref=src, dst_ref=dst, send_sem=self.send_sem.at[k], recv_sem=self.recv_sem.at[k],
            device_id=to, device_id_type=MESH,
        )
        copy.start()
        self.sent.append(copy)

    def wait(self, key, dst):
        k = self.index(key)
        pltpu.make_async_remote_copy(
            src_ref=dst, dst_ref=dst, send_sem=self.send_sem.at[k], recv_sem=self.recv_sem.at[k],
            device_id=place_id(), device_id_type=MESH,
        ).wait_recv()

    def drain(self):
        for copy in self.sent:
            copy.wait_send()


def place_id():
    return (lax.axis_index("fsdp"), lax.axis_index("ep"))


def part(kind, ref, p=None, h=None):
    if p is None:
        return ref
    size = (32 if kind == "in" else 1024) // (1 if h is None else 2)
    start = (32 if kind == "in" else 1024) * p + size * (h or 0)
    if kind == "in":
        return ref.at[pl.ds(start, size), :]
    return ref.at[:, pl.ds(start, size)]


def exchange_targets(x, y, z, c):
    out = []
    for kind, off in ((0, 0), (1, 1), (2, 7), (3, 2 + 4 * c)):
        for k in (0, 1):
            out.append((kind, k, rem(z + off, 8)))
    return out


def dot(left, right, dims=((1,), (0,))):
    return lax.dot_general(left, right, (dims, ((), ())), preferred_element_type=F32)


def ds(index, size):
    return pl.ds(pl.multiple_of(index * size, size), size)


def rows_of(ref, cols=None):
    if cols is None:
        return ref[...].reshape(ROWS, D)
    return ref[:, :, cols].reshape(ROWS, cols.size)


def kernel(tok_hbm, cot_hbm, rt, rw, win, wdn, layer, gtok, gin, gdn,
           tok, cot, fin, fdn, wd, sx, sdy, rx, rdy, ox, odx, box, bdx,
           back, whi, wlo, xt, gu, gh, hid, hidt, ggu,
           tin, tdn, a_in, a_dn, b_in, b_dn, c_in, c_dn, d_in, d_dn, e_in, e_dn,
           send_sem, recv_sem, a_send, a_recv, send_sem2, recv_sem2, r_send, r_recv, local_sem):
    x, y, z, c = place()
    zh = div(z, 4)
    e = lax.axis_index("ep")
    greet(x, y, z, c)
    link = Link(send_sem, recv_sem, N_SEM_A)
    full = {"in": fin, "dn": fdn}
    own = {"in": win, "dn": wdn}
    kinds = ("dn", "in")
    zs = (zh, 1 - zh)
    to_x = {s: device(rem(x + s, 4), y, z, c) for s in (1, 3)}
    to_y = {s: device(x, rem(y + s, 4), z, c) for s in (1, 3)}
    partner = device(x, y, rem(z + 4, 8), c)

    def slot(kind, q, xo, yo, p=None, h=None):
        return part(kind, full[kind].at[zs[q], rem(x + xo, 4), rem(y + yo, 4)], p, h)

    def start(q):
        for kind in kinds:
            src = own[kind] if q == 0 else slot(kind, q, 0, 0)
            for s in (1, 3):
                link.send(("x0", q, kind, s), src, slot(kind, q, 0, 0), to_x[s])
                link.send(("y0", q, kind, s), src, slot(kind, q, 0, 0), to_y[s])

    def first(q):
        for kind in kinds:
            for s in (1, 3):
                h = 0 if s == 1 else 1
                link.wait(("x0", q, kind, s), slot(kind, q, 4 - s, 0))
                for p in (0, 1):
                    piece = slot(kind, q, 4 - s, 0, p, h)
                    link.send(("xf", q, kind, p, 0, s), piece, piece, to_x[s])
                for t in (1, 3):
                    piece = slot(kind, q, 4 - s, 0, 0)
                    link.send(("y2", q, kind, 4 - s, t), piece, piece, to_y[t])
                link.wait(("y0", q, kind, s), slot(kind, q, 0, 4 - s))
                for p in (0, 1):
                    piece = slot(kind, q, 0, 4 - s, p, h)
                    link.send(("yf", q, kind, p, 0, s), piece, piece, to_y[s])
                for t in (1, 3):
                    piece = slot(kind, q, 0, 4 - s, 1)
                    link.send(("x2", q, kind, 4 - s, t), piece, piece, to_x[t])

    def second(q):
        for kind in kinds:
            for s in (1, 3):
                h = 0 if s == 1 else 1
                link.wait(("xf", q, kind, 0, 0, s), slot(kind, q, 2, 0, 0, h))
                link.wait(("yf", q, kind, 1, 0, s), slot(kind, q, 0, 2, 1, h))
            for t in (1, 3):
                piece = slot(kind, q, 2, 0, 0)
                link.send(("y2", q, kind, 2, t), piece, piece, to_y[t])
                piece = slot(kind, q, 0, 2, 1)
                link.send(("x2", q, kind, 2, t), piece, piece, to_x[t])

    def third(q, offsets):
        for kind in kinds:
            for o in offsets:
                for s in (1, 3):
                    h = 0 if s == 1 else 1
                    link.wait(("y2", q, kind, o, s), slot(kind, q, o, 4 - s, 0))
                    piece = slot(kind, q, o, 4 - s, 0, h)
                    link.send(("yf", q, kind, 0, o, s), piece, piece, to_y[s])
                    link.wait(("x2", q, kind, o, s), slot(kind, q, 4 - s, o, 1))
                    piece = slot(kind, q, 4 - s, o, 1, h)
                    link.send(("xf", q, kind, 1, o, s), piece, piece, to_x[s])

    def last(q, kind):
        for s in (1, 3):
            h = 0 if s == 1 else 1
            for o in range(4):
                link.wait(("yf", q, kind, 0, o, s), slot(kind, q, o, 2, 0, h))
                link.wait(("xf", q, kind, 1, o, s), slot(kind, q, 2, o, 1, h))

    for kind in kinds:
        link.send(("z", kind), own[kind], slot(kind, 0, 0, 0), partner)
    start(0)
    loads = []
    for n, (src, dst) in enumerate(((tok_hbm, tok), (cot_hbm, cot), (wdn, slot("dn", 0, 0, 0)), (win, slot("in", 0, 0, 0)))):
        copy = pltpu.make_async_copy(src, dst, local_sem.at[n])
        copy.start()
        loads.append(copy)

    experts = lax.broadcasted_iota(jnp.int32, (8, 128), 0)
    member = jnp.zeros((8, 128), F32)
    coef = jnp.zeros((8, 128), F32)
    for k in range(6):
        hit = jnp.broadcast_to(rt[k:k + 1, :], (8, 128)) == experts
        member = member + jnp.where(hit, 1.0, 0.0)
        coef = coef + jnp.where(hit, jnp.broadcast_to(rw[k:k + 1, :], (8, 128)), 0.0)
    before = lax.broadcasted_iota(jnp.int32, (128, 128), 0) < lax.broadcasted_iota(jnp.int32, (128, 128), 1)
    rank = dot(jnp.where(member > 0.5, 1.0, 0.0).astype(BF16), jnp.where(before, 1.0, 0.0).astype(BF16))
    rank = jnp.where(member > 0.5, rank, -1.0)
    ids = lax.broadcasted_iota(jnp.int32, (CAP, 128), 0).astype(F32)
    for copy in loads[:2]:
        copy.wait()
    tok_v, cot_v = tok[...], cot[...]
    for k in range(8):
        hits = jnp.broadcast_to(rank[k:k + 1, :], (CAP, 128)) == ids
        pick = jnp.where(hits, 1.0, 0.0)
        weight = jnp.where(hits, jnp.broadcast_to(coef[k:k + 1, :], (CAP, 128)), 0.0)
        sx[k] = dot(pick.astype(BF16), tok_v).astype(BF16)
        sdy[k] = (dot(pick.astype(BF16), cot_v) * jnp.sum(weight, axis=1, keepdims=True)).astype(BF16)
        high = weight.astype(BF16)
        back[pl.ds(CAP * k, CAP), :] = pick.astype(BF16)
        whi[pl.ds(CAP * k, CAP), :] = high
        wlo[pl.ds(CAP * k, CAP), :] = (weight - high.astype(F32)).astype(BF16)
    mine = rem(z, 4) * 2 + c
    rx[c] = sx[mine]
    rdy[c] = sdy[mine]

    first(0)
    for kind in kinds:
        link.wait(("z", kind), slot(kind, 1, 0, 0))
    start(1)
    rows = []
    for which, (src, dst) in enumerate(((sx, rx), (sdy, rdy))):
        for kind, k, zd in exchange_targets(x, y, z, c):
            if kind == 0:
                if k:
                    continue
                core = 1 - c
            else:
                core = k
            expert = rem(zd, 4) * 2 + core
            copy = pltpu.make_async_remote_copy(
                src_ref=src.at[expert], dst_ref=dst.at[2 * kind + c], send_sem=a_send.at[which * 8 + 2 * kind + k],
                recv_sem=a_recv.at[which * 8 + 2 * kind + c], device_id=device(x, y, zd, core), device_id_type=MESH,
            )
            copy.start()
            rows.append(copy)
    second(0)
    third(0, (1, 3))
    first(1)
    third(0, (2,))
    second(1)
    third(1, (1, 3))
    for which, dst in enumerate((rx, rdy)):
        for number in range(1, 8):
            s = number if number > 1 else 1 - c
            pltpu.make_async_remote_copy(
                src_ref=dst.at[s], dst_ref=dst.at[s], send_sem=a_send.at[which * 8 + number],
                recv_sem=a_recv.at[which * 8 + s], device_id=place_id(), device_id_type=MESH,
            ).wait_recv()
    third(1, (2,))
    for copy in loads[2:]:
        copy.wait()
    last(0, "dn")
    last(0, "in")

    @pl.loop(0, 8)
    def _(n):
        xt[ds(n, 256), :] = rows_of(rx, ds(n, 256)).T

    def gates(q):
        xs = rows_of(rx, ds(zs[q], 1024))

        @pl.loop(0, 6)
        def _(n):
            cols = ds(n, 256)
            value = dot(xs, fin[zs[q], :, :, :, cols].reshape(1024, 256))
            gu[:, cols] = value if q == 0 else gu[:, cols] + value

    gates(0)
    last(1, "dn")

    @pl.loop(0, 8)
    def _(g):
        for n in range(4):
            cols = pl.ds(512 * n, 512)
            wd[ds(g, 96), cols] = fdn[div(g, 4), rem(g, 4), :, :, cols].astype(F32).reshape(96, 512).astype(BF16)

    dy = rows_of(rdy)

    @pl.loop(0, 3)
    def _(n):
        gh[:, ds(n, 256)] = dot(dy, wd[ds(n, 256), :], ((1,), (1,)))

    last(1, "in")
    gates(1)

    @pl.loop(0, 3)
    def _(n):
        cols = ds(n, 256)
        ups = pl.ds(pl.multiple_of(FF + n * 256, 256), 256)
        gate, up, grad = gu[:, cols], gu[:, ups], gh[:, cols]
        sig = jax.nn.sigmoid(gate)
        act = gate * sig
        hidden = (act * up).astype(BF16)
        hid[:, cols] = hidden
        hidt[cols, :] = hidden.T
        ggu[:, cols] = (grad * up * sig * (1.0 + gate * (1.0 - sig))).astype(BF16)
        ggu[:, ups] = (grad * act).astype(BF16)

    zr = (1 - zh, zh)
    link2 = Link(send_sem2, recv_sem2, N_SEM_B)
    term = {"in": tin, "dn": tdn}
    buf_a = {"in": a_in, "dn": a_dn}
    buf_b = {"in": b_in, "dn": b_dn}
    buf_c = {"in": c_in, "dn": c_dn}
    buf_d = {"in": d_in, "dn": d_dn}
    buf_e = {"in": e_in, "dn": e_dn}
    to = {0: to_y, 1: to_x}
    offsets = (2, 1, 3, 0)

    def terms(q, kind):
        if kind == "dn":
            left = hidt[ds(zr[q], 384), :]

            @pl.loop(0, 4)
            def _(n):
                cols = ds(n, 512)
                tdn[zr[q], :, :, :, cols] = dot(left, rows_of(rdy, cols)).reshape(4, 4, 24, 512).astype(BF16)
        else:
            @pl.loop(0, 4)
            def _(i):
                left = xt[ds(zr[q] * 4 + i, 256), :]
                for n in range(3):
                    cols = pl.ds(512 * n, 512)
                    tin[zr[q], i, :, :, cols] = dot(left, ggu[:, cols]).astype(BF16).reshape(4, 64, 512)

    def block(kind, q, p, ring, other, h=None):
        xo, yo = (other, ring) if p == 0 else (ring, other)
        return part(kind, term[kind].at[zr[q], rem(x + xo, 4), rem(y + yo, 4)], p, h)

    def add(dst, *srcs):
        total = dst[...].astype(F32)
        for src in srcs:
            total = total + src[...].astype(F32)
        dst[...] = total.astype(BF16)

    def r1(q, kind):
        for o in offsets:
            for p in (0, 1):
                for s, h in ((3, 0), (1, 1)):
                    link2.send(("a", q, kind, p, o, s), block(kind, q, p, 2, o, h),
                               buf_a[kind].at[p, q, o, h], to[p][s])

    def r2(q):
        for kind in kinds:
            for o in offsets:
                for p in (0, 1):
                    for s, h in ((3, 0), (1, 1)):
                        link2.wait(("a", q, kind, p, o, s), buf_a[kind].at[p, q, o, h])
                        add(block(kind, q, p, s, o, h), buf_a[kind].at[p, q, o, h])
                        link2.send(("b", q, kind, p, o, s), block(kind, q, p, s, o),
                                   buf_b[kind].at[p, q, o, h], to[p][s])

    def r3(q):
        for kind in kinds:
            for o in offsets:
                for p in (0, 1):
                    for s, h in ((3, 0), (1, 1)):
                        link2.wait(("b", q, kind, p, o, s), buf_b[kind].at[p, q, o, h])
                    add(block(kind, q, p, 0, o), buf_b[kind].at[p, q, o, 0], buf_b[kind].at[p, q, o, 1])
                    if o == 2:
                        for s, h in ((3, 0), (1, 1)):
                            link2.send(("c", q, kind, p, s), block(kind, q, p, 0, 2, h),
                                       buf_c[kind].at[p, q, h], to[1 - p][s])
            for s, h in ((3, 0), (1, 1)):
                for p in (0, 1):
                    link2.wait(("c", q, kind, p, s), buf_c[kind].at[p, q, h])
                    add(block(kind, q, p, 0, s, h), buf_c[kind].at[p, q, h])
                    link2.send(("d", q, kind, p, s), block(kind, q, p, 0, s), buf_d[kind].at[p, q, h], to[1 - p][s])

    def wait_d(q, kind):
        for p in (0, 1):
            for s, h in ((3, 0), (1, 1)):
                link2.wait(("d", q, kind, p, s), buf_d[kind].at[p, q, h])

    def r4(q):
        for kind in kinds:
            wait_d(q, kind)
            for p in (0, 1):
                add(block(kind, q, p, 0, 0), buf_d[kind].at[p, q, 0], buf_d[kind].at[p, q, 1])
            link2.send(("e", kind), term[kind].at[zr[0], x, y], buf_e[kind], partner)

    for q in (0, 1):
        for kind in kinds:
            terms(q, kind)
            r1(q, kind)

    def rows_back(which, src, dst):
        for number in range(1, 8):
            if number == 1:
                s, zd, core = 1 - c, z, 1 - c
            else:
                off = {2: 7, 3: 7, 4: 1, 5: 1, 6: 6, 7: 2}[number]
                s, zd, core = number, rem(z + off, 8), number % 2
            copy = pltpu.make_async_remote_copy(
                src_ref=src.at[s], dst_ref=dst.at[e], send_sem=r_send.at[which * 8 + number],
                recv_sem=r_recv.at[which * 8 + 2 * (number // 2) + c], device_id=device(x, y, zd, core),
                device_id_type=MESH,
            )
            copy.start()
            rows.append(copy)
        dst[e] = src[c]

    hidden = hid[...]

    @pl.loop(0, 8)
    def _(n):
        cols = ds(n, 256)
        ox[:, :, cols] = dot(hidden, wd[:, cols]).astype(BF16).reshape(8, CAP, 256)

    rows_back(0, ox, box)
    gated = ggu[...]

    @pl.loop(0, 8)
    def _(g):
        value = dot(gated, fin[div(g, 4), rem(g, 4)].reshape(256, 2 * FF), ((1,), (1,)))
        odx[:, :, ds(g, 256)] = value.astype(BF16).reshape(8, CAP, 256)

    rows_back(1, odx, bdx)
    r2(0)
    r2(1)
    r3(0)
    r4(0)
    for which, dst in enumerate((box, bdx)):
        for kind, k, zd in exchange_targets(x, y, z, c):
            if kind == 0:
                if k:
                    continue
                core = 1 - c
            else:
                core = k
            expert = rem(zd, 4) * 2 + core
            pltpu.make_async_remote_copy(
                src_ref=dst.at[expert], dst_ref=dst.at[expert], send_sem=r_send.at[which * 8 + 1],
                recv_sem=r_recv.at[which * 8 + 2 * kind + core], device_id=place_id(), device_id_type=MESH,
            ).wait_recv()
    back_t, high_t, low_t = back[...].T, whi[...].T, wlo[...].T

    @pl.loop(0, 4)
    def _(n):
        cols = ds(n, 512)
        value = rows_of(box, cols)
        layer[:, cols] = (dot(high_t, value) + dot(low_t, value)).astype(BF16)
        gtok[:, cols] = dot(back_t, rows_of(bdx, cols)).astype(BF16)

    r3(1)
    for kind, out in (("dn", gdn), ("in", gin)):
        wait_d(1, kind)
        link2.wait(("e", kind), buf_e[kind])
        for p in (0, 1):
            total = block(kind, 1, p, 0, 0)[...].astype(F32) + buf_d[kind][p, 1, 0].astype(F32)
            total = total + buf_d[kind][p, 1, 1].astype(F32)
            total = total + part(kind, buf_e[kind], p)[...].astype(F32)
            part(kind, out, p)[...] = total
    for copy in rows:
        copy.wait_send()
    link.drain()
    link2.drain()


def call(tokens, cotangent, routes, weights, win, wdn):
    anyspace = pl.BlockSpec(memory_space=pl.ANY)
    vmem = pl.BlockSpec(memory_space=pltpu.VMEM)
    rows = pltpu.VMEM((8, CAP, D), BF16)
    return pl.pallas_call(
        kernel,
        name="expert_window",
        out_shape=(
            jax.ShapeDtypeStruct((128, D), BF16),
            jax.ShapeDtypeStruct((128, D), BF16),
            jax.ShapeDtypeStruct((64, 2 * FF), F32),
            jax.ShapeDtypeStruct((24, D), F32),
        ),
        in_specs=[anyspace, anyspace, vmem, vmem, anyspace, anyspace],
        out_specs=[vmem] * 4,
        scratch_shapes=[
            pltpu.VMEM((128, D), BF16),
            pltpu.VMEM((128, D), BF16),
            pltpu.VMEM((2, 4, 4, 64, 2 * FF), BF16),
            pltpu.VMEM((2, 4, 4, 24, D), BF16),
            pltpu.VMEM((FF, D), BF16),
            rows, rows, rows, rows, rows, rows, rows, rows,
            pltpu.VMEM((ROWS, 128), BF16),
            pltpu.VMEM((ROWS, 128), BF16),
            pltpu.VMEM((ROWS, 128), BF16),
            pltpu.VMEM((D, ROWS), BF16),
            pltpu.VMEM((ROWS, 2 * FF), F32),
            pltpu.VMEM((ROWS, FF), F32),
            pltpu.VMEM((ROWS, FF), BF16),
            pltpu.VMEM((FF, ROWS), BF16),
            pltpu.VMEM((ROWS, 2 * FF), BF16),
            pltpu.VMEM((2, 4, 4, 64, 2 * FF), BF16),
            pltpu.VMEM((2, 4, 4, 24, D), BF16),
            pltpu.VMEM((2, 2, 4, 2, 16, 2 * FF), BF16),
            pltpu.VMEM((2, 2, 4, 2, 24, 512), BF16),
            pltpu.VMEM((2, 2, 4, 2, 32, 2 * FF), BF16),
            pltpu.VMEM((2, 2, 4, 2, 24, 1024), BF16),
            pltpu.VMEM((2, 2, 2, 16, 2 * FF), BF16),
            pltpu.VMEM((2, 2, 2, 24, 512), BF16),
            pltpu.VMEM((2, 2, 2, 32, 2 * FF), BF16),
            pltpu.VMEM((2, 2, 2, 24, 1024), BF16),
            pltpu.VMEM((64, 2 * FF), BF16),
            pltpu.VMEM((24, D), BF16),
            pltpu.SemaphoreType.DMA((N_SEM_A,)),
            pltpu.SemaphoreType.DMA((N_SEM_A,)),
            pltpu.SemaphoreType.DMA((16,)),
            pltpu.SemaphoreType.DMA((16,)),
            pltpu.SemaphoreType.DMA((N_SEM_B,)),
            pltpu.SemaphoreType.DMA((N_SEM_B,)),
            pltpu.SemaphoreType.DMA((16,)),
            pltpu.SemaphoreType.DMA((16,)),
            pltpu.SemaphoreType.DMA((4,)),
        ],
        compiler_params=pltpu.CompilerParams(
            collective_id=0, has_side_effects=True, vmem_limit_bytes=60 * 1024 * 1024
        ),
    )(tokens, cotangent, routes, weights, win, wdn)


def local(tokens, routes, route_weight, w_in, w_down, cotangent):
    layer_out, grad_tokens, grad_in, grad_down = call(
        tokens, cotangent, routes.T, route_weight.T, w_in[0].reshape(64, 2 * FF), w_down[0]
    )
    return layer_out, grad_tokens, grad_in.reshape(w_in.shape), grad_down.reshape(w_down.shape)


def solution(mesh):
    in_specs = (
        P(("fsdp", "ep"), None),
        P(("fsdp", "ep"), None),
        P(("fsdp", "ep"), None),
        P("ep", "fsdp", None, None),
        P("ep", "fsdp", None),
        P(("fsdp", "ep"), None),
    )
    out_specs = (
        P(("fsdp", "ep"), None),
        P(("fsdp", "ep"), None),
        P("ep", "fsdp", None, None),
        P("ep", "fsdp", None),
    )
    return jax.shard_map(local, mesh=mesh, in_specs=in_specs, out_specs=out_specs, check_vma=False)
```

```python
import jax
import jax.numpy as jnp
from jax import lax
from jax.experimental import pallas as pl
from jax.experimental.pallas import tpu as pltpu
from jax.sharding import PartitionSpec as P

D = 2048
FF = 768
CAP = 32
MESH = pl.DeviceIdType.MESH
F32 = jnp.float32
BF16 = jnp.bfloat16
N_SEM_A = 200
N_SEM_B = 220
ROWS = 8 * CAP


def rem(value, modulus):
    return lax.rem(value, jnp.int32(modulus))


def div(value, divisor):
    return lax.div(value, jnp.int32(divisor))


def place():
    f = lax.axis_index("fsdp")
    e = lax.axis_index("ep")
    return rem(div(f, 4), 4), rem(f, 4), div(f, 16) * 4 + div(e, 2), rem(e, 2)


def device(x, y, z, c):
    return (div(z, 4) * 16 + x * 4 + y, rem(z, 4) * 2 + c)


def greet(x, y, z, c):
    barrier = pltpu.get_barrier_semaphore()
    peers = [device(rem(x + o, 4), y, z, c) for o in (1, 3)]
    peers += [device(x, rem(y + o, 4), z, c) for o in (1, 3)]
    peers += [device(x, y, rem(z + 4, 8), c), device(x, y, z, 1 - c)]
    peers += [device(x, y, rem(z + o, 8), k) for o in (1, 7, 2, 6) for k in (0, 1)]
    for peer in peers:
        pl.semaphore_signal(barrier, inc=1, device_id=peer, device_id_type=MESH)
    pl.semaphore_wait(barrier, len(peers))


class Link:
    def __init__(self, send_sem, recv_sem, limit):
        self.send_sem, self.recv_sem, self.limit = send_sem, recv_sem, limit
        self.number, self.sent = {}, []

    def index(self, key):
        number = self.number.setdefault(key, len(self.number))
        assert number < self.limit
        return number

    def send(self, key, src, dst, to):
        k = self.index(key)
        copy = pltpu.make_async_remote_copy(
            src_ref=src, dst_ref=dst, send_sem=self.send_sem.at[k], recv_sem=self.recv_sem.at[k],
            device_id=to, device_id_type=MESH,
        )
        copy.start()
        self.sent.append(copy)

    def wait(self, key, dst):
        k = self.index(key)
        pltpu.make_async_remote_copy(
            src_ref=dst, dst_ref=dst, send_sem=self.send_sem.at[k], recv_sem=self.recv_sem.at[k],
            device_id=place_id(), device_id_type=MESH,
        ).wait_recv()

    def drain(self):
        for copy in self.sent:
            copy.wait_send()


def place_id():
    return (lax.axis_index("fsdp"), lax.axis_index("ep"))


def part(kind, ref, p=None, h=None):
    if p is None:
        return ref
    size = (32 if kind == "in" else 1024) // (1 if h is None else 2)
    start = (32 if kind == "in" else 1024) * p + size * (h or 0)
    if kind == "in":
        return ref.at[pl.ds(start, size), :]
    return ref.at[:, pl.ds(start, size)]


def exchange_targets(x, y, z, c):
    out = []
    for kind, off in ((0, 0), (1, 1), (2, 7), (3, 2 + 4 * c)):
        for k in (0, 1):
            out.append((kind, k, rem(z + off, 8)))
    return out


def dot(left, right, dims=((1,), (0,))):
    return lax.dot_general(left, right, (dims, ((), ())), preferred_element_type=F32)


def ds(index, size):
    return pl.ds(pl.multiple_of(index * size, size), size)


def rows_of(ref, cols=None):
    if cols is None:
        return ref[...].reshape(ROWS, D)
    return ref[:, :, cols].reshape(ROWS, cols.size)


def kernel(tok_hbm, cot_hbm, rt, rw, win, wdn, layer, gtok, gin, gdn,
           tok, cot, fin, fdn, wd, sx, sdy, rx, rdy, ox, odx, box, bdx,
           back, whi, wlo, xt, gu, gh, hid, hidt, ggu,
           tin, tdn, a_in, a_dn, b_in, b_dn, c_in, c_dn, d_in, d_dn, e_in, e_dn,
           send_sem, recv_sem, a_send, a_recv, send_sem2, recv_sem2, r_send, r_recv, local_sem):
    x, y, z, c = place()
    zh = div(z, 4)
    e = lax.axis_index("ep")
    greet(x, y, z, c)
    link = Link(send_sem, recv_sem, N_SEM_A)
    full = {"in": fin, "dn": fdn}
    own = {"in": win, "dn": wdn}
    zs = (zh, 1 - zh)
    to_x = {s: device(rem(x + s, 4), y, z, c) for s in (1, 3)}
    to_y = {s: device(x, rem(y + s, 4), z, c) for s in (1, 3)}
    partner = device(x, y, rem(z + 4, 8), c)

    def slot(kind, q, xo, yo, p=None, h=None):
        return part(kind, full[kind].at[zs[q], rem(x + xo, 4), rem(y + yo, 4)], p, h)

    def start(q, kind):
        src = own[kind] if q == 0 else slot(kind, q, 0, 0)
        for s in (1, 3):
            link.send(("x0", q, kind, s), src, slot(kind, q, 0, 0), to_x[s])
            link.send(("y0", q, kind, s), src, slot(kind, q, 0, 0), to_y[s])

    def first(q, kind):
        for s in (1, 3):
            h = 0 if s == 1 else 1
            link.wait(("x0", q, kind, s), slot(kind, q, 4 - s, 0))
            for p in (0, 1):
                piece = slot(kind, q, 4 - s, 0, p, h)
                link.send(("xf", q, kind, p, 0, s), piece, piece, to_x[s])
            for t in (1, 3):
                piece = slot(kind, q, 4 - s, 0, 0)
                link.send(("y2", q, kind, 4 - s, t), piece, piece, to_y[t])
            link.wait(("y0", q, kind, s), slot(kind, q, 0, 4 - s))
            for p in (0, 1):
                piece = slot(kind, q, 0, 4 - s, p, h)
                link.send(("yf", q, kind, p, 0, s), piece, piece, to_y[s])
            for t in (1, 3):
                piece = slot(kind, q, 0, 4 - s, 1)
                link.send(("x2", q, kind, 4 - s, t), piece, piece, to_x[t])

    def second(q, kind):
        for s in (1, 3):
            h = 0 if s == 1 else 1
            link.wait(("xf", q, kind, 0, 0, s), slot(kind, q, 2, 0, 0, h))
            link.wait(("yf", q, kind, 1, 0, s), slot(kind, q, 0, 2, 1, h))
        for t in (1, 3):
            piece = slot(kind, q, 2, 0, 0)
            link.send(("y2", q, kind, 2, t), piece, piece, to_y[t])
            piece = slot(kind, q, 0, 2, 1)
            link.send(("x2", q, kind, 2, t), piece, piece, to_x[t])

    def third(q, kind, offsets):
        for o in offsets:
            for s in (1, 3):
                h = 0 if s == 1 else 1
                link.wait(("y2", q, kind, o, s), slot(kind, q, o, 4 - s, 0))
                piece = slot(kind, q, o, 4 - s, 0, h)
                link.send(("yf", q, kind, 0, o, s), piece, piece, to_y[s])
                link.wait(("x2", q, kind, o, s), slot(kind, q, 4 - s, o, 1))
                piece = slot(kind, q, 4 - s, o, 1, h)
                link.send(("xf", q, kind, 1, o, s), piece, piece, to_x[s])

    def last(q, kind):
        for s in (1, 3):
            h = 0 if s == 1 else 1
            for o in range(4):
                link.wait(("yf", q, kind, 0, o, s), slot(kind, q, o, 2, 0, h))
                link.wait(("xf", q, kind, 1, o, s), slot(kind, q, 2, o, 1, h))

    for kind in ("in", "dn"):
        link.send(("z", kind), own[kind], slot(kind, 0, 0, 0), partner)
    start(0, "in")
    loads = []
    for n, (src, dst) in enumerate(((tok_hbm, tok), (cot_hbm, cot), (wdn, slot("dn", 0, 0, 0)), (win, slot("in", 0, 0, 0)))):
        copy = pltpu.make_async_copy(src, dst, local_sem.at[n])
        copy.start()
        loads.append(copy)

    experts = lax.broadcasted_iota(jnp.int32, (8, 128), 0)
    member = jnp.zeros((8, 128), F32)
    coef = jnp.zeros((8, 128), F32)
    for k in range(6):
        hit = jnp.broadcast_to(rt[k:k + 1, :], (8, 128)) == experts
        member = member + jnp.where(hit, 1.0, 0.0)
        coef = coef + jnp.where(hit, jnp.broadcast_to(rw[k:k + 1, :], (8, 128)), 0.0)
    before = lax.broadcasted_iota(jnp.int32, (128, 128), 0) < lax.broadcasted_iota(jnp.int32, (128, 128), 1)
    rank = dot(jnp.where(member > 0.5, 1.0, 0.0).astype(BF16), jnp.where(before, 1.0, 0.0).astype(BF16))
    rank = jnp.where(member > 0.5, rank, -1.0)
    ids = lax.broadcasted_iota(jnp.int32, (CAP, 128), 0).astype(F32)
    for copy in loads[:2]:
        copy.wait()
    tok_v, cot_v = tok[...], cot[...]
    for k in range(8):
        hits = jnp.broadcast_to(rank[k:k + 1, :], (CAP, 128)) == ids
        pick = jnp.where(hits, 1.0, 0.0)
        weight = jnp.where(hits, jnp.broadcast_to(coef[k:k + 1, :], (CAP, 128)), 0.0)
        sx[k] = dot(pick.astype(BF16), tok_v).astype(BF16)
        sdy[k] = (dot(pick.astype(BF16), cot_v) * jnp.sum(weight, axis=1, keepdims=True)).astype(BF16)
        high = weight.astype(BF16)
        back[pl.ds(CAP * k, CAP), :] = pick.astype(BF16)
        whi[pl.ds(CAP * k, CAP), :] = high
        wlo[pl.ds(CAP * k, CAP), :] = (weight - high.astype(F32)).astype(BF16)
    mine = rem(z, 4) * 2 + c
    rx[c] = sx[mine]
    rdy[c] = sdy[mine]

    first(0, "in")
    second(0, "in")
    link.wait(("z", "in"), slot("in", 1, 0, 0))
    start(1, "in")
    rows = []
    for which, (src, dst) in enumerate(((sx, rx), (sdy, rdy))):
        for kind, k, zd in exchange_targets(x, y, z, c):
            if kind == 0:
                if k:
                    continue
                core = 1 - c
            else:
                core = k
            expert = rem(zd, 4) * 2 + core
            copy = pltpu.make_async_remote_copy(
                src_ref=src.at[expert], dst_ref=dst.at[2 * kind + c], send_sem=a_send.at[which * 8 + 2 * kind + k],
                recv_sem=a_recv.at[which * 8 + 2 * kind + c], device_id=device(x, y, zd, core), device_id_type=MESH,
            )
            copy.start()
            rows.append(copy)
    third(0, "in", (1, 3))
    start(0, "dn")
    first(1, "in")
    third(0, "in", (2,))
    link.wait(("z", "dn"), slot("dn", 1, 0, 0))
    start(1, "dn")
    second(1, "in")
    first(0, "dn")
    third(1, "in", (1, 3))
    first(1, "dn")
    second(0, "dn")
    third(1, "in", (2,))
    second(1, "dn")

    def rows_here(which, dst):
        for number in range(1, 8):
            s = number if number > 1 else 1 - c
            pltpu.make_async_remote_copy(
                src_ref=dst.at[s], dst_ref=dst.at[s], send_sem=a_send.at[which * 8 + number],
                recv_sem=a_recv.at[which * 8 + s], device_id=place_id(), device_id_type=MESH,
            ).wait_recv()

    def gates(q):
        xs = rows_of(rx, ds(zs[q], 1024))

        @pl.loop(0, 6)
        def _(n):
            cols = ds(n, 256)
            value = dot(xs, fin[zs[q], :, :, :, cols].reshape(1024, 256))
            gu[:, cols] = value if q == 0 else gu[:, cols] + value

    for copy in loads[2:]:
        copy.wait()
    rows_here(0, rx)
    last(0, "in")
    gates(0)
    third(0, "dn", (1, 3))
    third(1, "dn", (1, 3))
    last(1, "in")
    gates(1)
    third(0, "dn", (2,))
    third(1, "dn", (2,))

    @pl.loop(0, 3)
    def _(n):
        cols = ds(n, 256)
        ups = pl.ds(pl.multiple_of(FF + n * 256, 256), 256)
        gate = gu[:, cols]
        hidden = (gate * jax.nn.sigmoid(gate) * gu[:, ups]).astype(BF16)
        hid[:, cols] = hidden
        hidt[cols, :] = hidden.T

    rows_here(1, rdy)

    zr = (1 - zh, zh)
    link2 = Link(send_sem2, recv_sem2, N_SEM_B)
    term = {"in": tin, "dn": tdn}
    buf_a = {"in": a_in, "dn": a_dn}
    buf_b = {"in": b_in, "dn": b_dn}
    buf_c = {"in": c_in, "dn": c_dn}
    buf_d = {"in": d_in, "dn": d_dn}
    buf_e = {"in": e_in, "dn": e_dn}
    to = {0: to_y, 1: to_x}
    offsets = (2, 1, 3, 0)

    def terms(q, kind):
        if kind == "dn":
            left = hidt[ds(zr[q], 384), :]

            @pl.loop(0, 4)
            def _(n):
                cols = ds(n, 512)
                tdn[zr[q], :, :, :, cols] = dot(left, rows_of(rdy, cols)).reshape(4, 4, 24, 512).astype(BF16)
        else:
            @pl.loop(0, 4)
            def _(i):
                left = xt[ds(zr[q] * 4 + i, 256), :]
                for n in range(3):
                    cols = pl.ds(512 * n, 512)
                    tin[zr[q], i, :, :, cols] = dot(left, ggu[:, cols]).astype(BF16).reshape(4, 64, 512)

    def block(kind, q, p, ring, other, h=None):
        xo, yo = (other, ring) if p == 0 else (ring, other)
        return part(kind, term[kind].at[zr[q], rem(x + xo, 4), rem(y + yo, 4)], p, h)

    def add(dst, *srcs):
        total = dst[...].astype(F32)
        for src in srcs:
            total = total + src[...].astype(F32)
        dst[...] = total.astype(BF16)

    def r1(q, kind):
        for o in offsets:
            for p in (0, 1):
                for s, h in ((3, 0), (1, 1)):
                    link2.send(("a", q, kind, p, o, s), block(kind, q, p, 2, o, h),
                               buf_a[kind].at[p, q, o, h], to[p][s])

    def r2(q, kind):
        for o in offsets:
            for p in (0, 1):
                for s, h in ((3, 0), (1, 1)):
                    link2.wait(("a", q, kind, p, o, s), buf_a[kind].at[p, q, o, h])
                    add(block(kind, q, p, s, o, h), buf_a[kind].at[p, q, o, h])
                    link2.send(("b", q, kind, p, o, s), block(kind, q, p, s, o),
                               buf_b[kind].at[p, q, o, h], to[p][s])

    def r3(q, kind):
        for o in offsets:
            for p in (0, 1):
                for s, h in ((3, 0), (1, 1)):
                    link2.wait(("b", q, kind, p, o, s), buf_b[kind].at[p, q, o, h])
                add(block(kind, q, p, 0, o), buf_b[kind].at[p, q, o, 0], buf_b[kind].at[p, q, o, 1])
                if o == 2:
                    for s, h in ((3, 0), (1, 1)):
                        link2.send(("c", q, kind, p, s), block(kind, q, p, 0, 2, h),
                                   buf_c[kind].at[p, q, h], to[1 - p][s])
        for s, h in ((3, 0), (1, 1)):
            for p in (0, 1):
                link2.wait(("c", q, kind, p, s), buf_c[kind].at[p, q, h])
                add(block(kind, q, p, 0, s, h), buf_c[kind].at[p, q, h])
                link2.send(("d", q, kind, p, s), block(kind, q, p, 0, s), buf_d[kind].at[p, q, h], to[1 - p][s])

    def wait_d(q, kind):
        for p in (0, 1):
            for s, h in ((3, 0), (1, 1)):
                link2.wait(("d", q, kind, p, s), buf_d[kind].at[p, q, h])

    def r4(q, kind):
        wait_d(q, kind)
        for p in (0, 1):
            add(block(kind, q, p, 0, 0), buf_d[kind].at[p, q, 0], buf_d[kind].at[p, q, 1])
        link2.send(("e", kind), term[kind].at[zr[0], x, y], buf_e[kind], partner)

    for q in (0, 1):
        terms(q, "dn")
        r1(q, "dn")

    last(0, "dn")
    last(1, "dn")

    @pl.loop(0, 8)
    def _(g):
        for n in range(4):
            cols = pl.ds(512 * n, 512)
            wd[ds(g, 96), cols] = fdn[div(g, 4), rem(g, 4), :, :, cols].astype(F32).reshape(96, 512).astype(BF16)

    r2(0, "dn")
    dy = rows_of(rdy)

    @pl.loop(0, 3)
    def _(n):
        gh[:, ds(n, 256)] = dot(dy, wd[ds(n, 256), :], ((1,), (1,)))

    @pl.loop(0, 3)
    def _(n):
        cols = ds(n, 256)
        ups = pl.ds(pl.multiple_of(FF + n * 256, 256), 256)
        gate, up, grad = gu[:, cols], gu[:, ups], gh[:, cols]
        sig = jax.nn.sigmoid(gate)
        ggu[:, cols] = (grad * up * sig * (1.0 + gate * (1.0 - sig))).astype(BF16)
        ggu[:, ups] = (grad * (gate * sig)).astype(BF16)

    @pl.loop(0, 8)
    def _(n):
        xt[ds(n, 256), :] = rows_of(rx, ds(n, 256)).T

    terms(0, "in")
    r1(0, "in")
    r2(1, "dn")
    terms(1, "in")
    r1(1, "in")

    def rows_back(which, src, dst):
        for number in range(1, 8):
            if number == 1:
                s, zd, core = 1 - c, z, 1 - c
            else:
                off = {2: 7, 3: 7, 4: 1, 5: 1, 6: 6, 7: 2}[number]
                s, zd, core = number, rem(z + off, 8), number % 2
            copy = pltpu.make_async_remote_copy(
                src_ref=src.at[s], dst_ref=dst.at[e], send_sem=r_send.at[which * 8 + number],
                recv_sem=r_recv.at[which * 8 + 2 * (number // 2) + c], device_id=device(x, y, zd, core),
                device_id_type=MESH,
            )
            copy.start()
            rows.append(copy)
        dst[e] = src[c]

    hidden = hid[...]

    @pl.loop(0, 8)
    def _(n):
        cols = ds(n, 256)
        ox[:, :, cols] = dot(hidden, wd[:, cols]).astype(BF16).reshape(8, CAP, 256)

    rows_back(0, ox, box)
    gated = ggu[...]

    @pl.loop(0, 8)
    def _(g):
        value = dot(gated, fin[div(g, 4), rem(g, 4)].reshape(256, 2 * FF), ((1,), (1,)))
        odx[:, :, ds(g, 256)] = value.astype(BF16).reshape(8, CAP, 256)

    rows_back(1, odx, bdx)
    r2(0, "in")
    r3(0, "dn")
    r2(1, "in")
    r4(0, "dn")
    r3(0, "in")
    r3(1, "dn")
    r4(0, "in")
    for which, dst in enumerate((box, bdx)):
        for kind, k, zd in exchange_targets(x, y, z, c):
            if kind == 0:
                if k:
                    continue
                core = 1 - c
            else:
                core = k
            expert = rem(zd, 4) * 2 + core
            pltpu.make_async_remote_copy(
                src_ref=dst.at[expert], dst_ref=dst.at[expert], send_sem=r_send.at[which * 8 + 1],
                recv_sem=r_recv.at[which * 8 + 2 * kind + core], device_id=place_id(), device_id_type=MESH,
            ).wait_recv()
    back_t, high_t, low_t = back[...].T, whi[...].T, wlo[...].T

    @pl.loop(0, 4)
    def _(n):
        cols = ds(n, 512)
        value = rows_of(box, cols)
        layer[:, cols] = (dot(high_t, value) + dot(low_t, value)).astype(BF16)
        gtok[:, cols] = dot(back_t, rows_of(bdx, cols)).astype(BF16)

    r3(1, "in")
    for kind, out in (("dn", gdn), ("in", gin)):
        wait_d(1, kind)
        link2.wait(("e", kind), buf_e[kind])
        for p in (0, 1):
            total = block(kind, 1, p, 0, 0)[...].astype(F32) + buf_d[kind][p, 1, 0].astype(F32)
            total = total + buf_d[kind][p, 1, 1].astype(F32)
            total = total + part(kind, buf_e[kind], p)[...].astype(F32)
            part(kind, out, p)[...] = total
    for copy in rows:
        copy.wait_send()
    link.drain()
    link2.drain()


def call(tokens, cotangent, routes, weights, win, wdn):
    anyspace = pl.BlockSpec(memory_space=pl.ANY)
    vmem = pl.BlockSpec(memory_space=pltpu.VMEM)
    rows = pltpu.VMEM((8, CAP, D), BF16)
    return pl.pallas_call(
        kernel,
        name="expert_window",
        out_shape=(
            jax.ShapeDtypeStruct((128, D), BF16),
            jax.ShapeDtypeStruct((128, D), BF16),
            jax.ShapeDtypeStruct((64, 2 * FF), F32),
            jax.ShapeDtypeStruct((24, D), F32),
        ),
        in_specs=[anyspace, anyspace, vmem, vmem, anyspace, anyspace],
        out_specs=[vmem] * 4,
        scratch_shapes=[
            pltpu.VMEM((128, D), BF16),
            pltpu.VMEM((128, D), BF16),
            pltpu.VMEM((2, 4, 4, 64, 2 * FF), BF16),
            pltpu.VMEM((2, 4, 4, 24, D), BF16),
            pltpu.VMEM((FF, D), BF16),
            rows, rows, rows, rows, rows, rows, rows, rows,
            pltpu.VMEM((ROWS, 128), BF16),
            pltpu.VMEM((ROWS, 128), BF16),
            pltpu.VMEM((ROWS, 128), BF16),
            pltpu.VMEM((D, ROWS), BF16),
            pltpu.VMEM((ROWS, 2 * FF), F32),
            pltpu.VMEM((ROWS, FF), F32),
            pltpu.VMEM((ROWS, FF), BF16),
            pltpu.VMEM((FF, ROWS), BF16),
            pltpu.VMEM((ROWS, 2 * FF), BF16),
            pltpu.VMEM((2, 4, 4, 64, 2 * FF), BF16),
            pltpu.VMEM((2, 4, 4, 24, D), BF16),
            pltpu.VMEM((2, 2, 4, 2, 16, 2 * FF), BF16),
            pltpu.VMEM((2, 2, 4, 2, 24, 512), BF16),
            pltpu.VMEM((2, 2, 4, 2, 32, 2 * FF), BF16),
            pltpu.VMEM((2, 2, 4, 2, 24, 1024), BF16),
            pltpu.VMEM((2, 2, 2, 16, 2 * FF), BF16),
            pltpu.VMEM((2, 2, 2, 24, 512), BF16),
            pltpu.VMEM((2, 2, 2, 32, 2 * FF), BF16),
            pltpu.VMEM((2, 2, 2, 24, 1024), BF16),
            pltpu.VMEM((64, 2 * FF), BF16),
            pltpu.VMEM((24, D), BF16),
            pltpu.SemaphoreType.DMA((N_SEM_A,)),
            pltpu.SemaphoreType.DMA((N_SEM_A,)),
            pltpu.SemaphoreType.DMA((16,)),
            pltpu.SemaphoreType.DMA((16,)),
            pltpu.SemaphoreType.DMA((N_SEM_B,)),
            pltpu.SemaphoreType.DMA((N_SEM_B,)),
            pltpu.SemaphoreType.DMA((16,)),
            pltpu.SemaphoreType.DMA((16,)),
            pltpu.SemaphoreType.DMA((4,)),
        ],
        compiler_params=pltpu.CompilerParams(
            collective_id=0, has_side_effects=True, vmem_limit_bytes=60 * 1024 * 1024
        ),
    )(tokens, cotangent, routes, weights, win, wdn)


def local(tokens, routes, route_weight, w_in, w_down, cotangent):
    layer_out, grad_tokens, grad_in, grad_down = call(
        tokens, cotangent, routes.T, route_weight.T, w_in[0].reshape(64, 2 * FF), w_down[0]
    )
    return layer_out, grad_tokens, grad_in.reshape(w_in.shape), grad_down.reshape(w_down.shape)


def solution(mesh):
    in_specs = (
        P(("fsdp", "ep"), None),
        P(("fsdp", "ep"), None),
        P(("fsdp", "ep"), None),
        P("ep", "fsdp", None, None),
        P("ep", "fsdp", None),
        P(("fsdp", "ep"), None),
    )
    out_specs = (
        P(("fsdp", "ep"), None),
        P(("fsdp", "ep"), None),
        P("ep", "fsdp", None, None),
        P("ep", "fsdp", None),
    )
    return jax.shard_map(local, mesh=mesh, in_specs=in_specs, out_specs=out_specs, check_vma=False)
```

```python
import jax
import jax.numpy as jnp
from jax import lax
from jax.experimental import pallas as pl
from jax.experimental.pallas import tpu as pltpu
from jax.sharding import PartitionSpec as P

D = 2048
FF = 768
CAP = 32
MESH = pl.DeviceIdType.MESH
F32 = jnp.float32
BF16 = jnp.bfloat16
N_SEM_A = 200
N_SEM_B = 220
ROWS = 8 * CAP


def rem(value, modulus):
    return lax.rem(value, jnp.int32(modulus))


def div(value, divisor):
    return lax.div(value, jnp.int32(divisor))


def place():
    f = lax.axis_index("fsdp")
    e = lax.axis_index("ep")
    return rem(div(f, 4), 4), rem(f, 4), div(f, 16) * 4 + div(e, 2), rem(e, 2)


def device(x, y, z, c):
    return (div(z, 4) * 16 + x * 4 + y, rem(z, 4) * 2 + c)


def greet(x, y, z, c):
    barrier = pltpu.get_barrier_semaphore()
    peers = [device(rem(x + o, 4), y, z, c) for o in (1, 3)]
    peers += [device(x, rem(y + o, 4), z, c) for o in (1, 3)]
    peers += [device(x, y, rem(z + 4, 8), c), device(x, y, z, 1 - c)]
    peers += [device(x, y, rem(z + o, 8), k) for o in (1, 7, 2, 6) for k in (0, 1)]
    for peer in peers:
        pl.semaphore_signal(barrier, inc=1, device_id=peer, device_id_type=MESH)
    pl.semaphore_wait(barrier, len(peers))


class Link:
    def __init__(self, send_sem, recv_sem, limit):
        self.send_sem, self.recv_sem, self.limit = send_sem, recv_sem, limit
        self.number, self.sent = {}, []

    def index(self, key):
        number = self.number.setdefault(key, len(self.number))
        assert number < self.limit
        return number

    def send(self, key, src, dst, to):
        k = self.index(key)
        copy = pltpu.make_async_remote_copy(
            src_ref=src, dst_ref=dst, send_sem=self.send_sem.at[k], recv_sem=self.recv_sem.at[k],
            device_id=to, device_id_type=MESH,
        )
        copy.start()
        self.sent.append(copy)

    def wait(self, key, dst):
        k = self.index(key)
        pltpu.make_async_remote_copy(
            src_ref=dst, dst_ref=dst, send_sem=self.send_sem.at[k], recv_sem=self.recv_sem.at[k],
            device_id=place_id(), device_id_type=MESH,
        ).wait_recv()

    def drain(self):
        for copy in self.sent:
            copy.wait_send()


def place_id():
    return (lax.axis_index("fsdp"), lax.axis_index("ep"))


def part(kind, ref, p=None, h=None):
    if p is None:
        return ref
    size = (32 if kind == "in" else 1024) // (1 if h is None else 2)
    start = (32 if kind == "in" else 1024) * p + size * (h or 0)
    if kind == "in":
        return ref.at[pl.ds(start, size), :]
    return ref.at[:, pl.ds(start, size)]


def exchange_targets(x, y, z, c):
    out = []
    for kind, off in ((0, 0), (1, 1), (2, 7), (3, 2 + 4 * c)):
        for k in (0, 1):
            out.append((kind, k, rem(z + off, 8)))
    return out


def dot(left, right, dims=((1,), (0,))):
    return lax.dot_general(left, right, (dims, ((), ())), preferred_element_type=F32)


def ds(index, size):
    return pl.ds(pl.multiple_of(index * size, size), size)


def rows_of(ref, cols=None):
    if cols is None:
        return ref[...].reshape(ROWS, D)
    return ref[:, :, cols].reshape(ROWS, cols.size)


def kernel(tok_hbm, cot_hbm, rt, rw, win, wdn, layer_hbm, gtok_hbm, gin_hbm, gdn_hbm,
           layer, gtok, gin, gdn, raw, flat, wide, tok, cot, fin, fdn, wd, sx, sdy, rx, rdy, ox, odx, box, bdx,
           back, whi, wlo, xt, gu, gh, hid, hidt, ggu,
           tin, tdn, a_in, a_dn, b_in, b_dn, c_in, c_dn, d_in, d_dn, e_in, e_dn,
           send_sem, recv_sem, a_send, a_recv, send_sem2, recv_sem2, r_send, r_recv, local_sem, out_sem):
    x, y, z, c = place()
    zh = div(z, 4)
    e = lax.axis_index("ep")
    fetch = pltpu.make_async_copy(win, raw, local_sem.at[3])
    fetch.start()
    greet(x, y, z, c)
    link = Link(send_sem, recv_sem, N_SEM_A)
    full = {"in": fin, "dn": fdn}
    own = {"in": flat, "dn": wdn}
    zs = (zh, 1 - zh)
    to_x = {s: device(rem(x + s, 4), y, z, c) for s in (1, 3)}
    to_y = {s: device(x, rem(y + s, 4), z, c) for s in (1, 3)}
    partner = device(x, y, rem(z + 4, 8), c)

    def slot(kind, q, xo, yo, p=None, h=None):
        return part(kind, full[kind].at[zs[q], rem(x + xo, 4), rem(y + yo, 4)], p, h)

    def start(q, kind):
        src = own[kind] if q == 0 else slot(kind, q, 0, 0)
        for s in (1, 3):
            link.send(("x0", q, kind, s), src, slot(kind, q, 0, 0), to_x[s])
            link.send(("y0", q, kind, s), src, slot(kind, q, 0, 0), to_y[s])

    def first(q, kind):
        for s in (1, 3):
            h = 0 if s == 1 else 1
            link.wait(("x0", q, kind, s), slot(kind, q, 4 - s, 0))
            for p in (0, 1):
                piece = slot(kind, q, 4 - s, 0, p, h)
                link.send(("xf", q, kind, p, 0, s), piece, piece, to_x[s])
            for t in (1, 3):
                piece = slot(kind, q, 4 - s, 0, 0)
                link.send(("y2", q, kind, 4 - s, t), piece, piece, to_y[t])
            link.wait(("y0", q, kind, s), slot(kind, q, 0, 4 - s))
            for p in (0, 1):
                piece = slot(kind, q, 0, 4 - s, p, h)
                link.send(("yf", q, kind, p, 0, s), piece, piece, to_y[s])
            for t in (1, 3):
                piece = slot(kind, q, 0, 4 - s, 1)
                link.send(("x2", q, kind, 4 - s, t), piece, piece, to_x[t])

    def second(q, kind):
        for s in (1, 3):
            h = 0 if s == 1 else 1
            link.wait(("xf", q, kind, 0, 0, s), slot(kind, q, 2, 0, 0, h))
            link.wait(("yf", q, kind, 1, 0, s), slot(kind, q, 0, 2, 1, h))
        for t in (1, 3):
            piece = slot(kind, q, 2, 0, 0)
            link.send(("y2", q, kind, 2, t), piece, piece, to_y[t])
            piece = slot(kind, q, 0, 2, 1)
            link.send(("x2", q, kind, 2, t), piece, piece, to_x[t])

    def third(q, kind, offsets):
        for o in offsets:
            for s in (1, 3):
                h = 0 if s == 1 else 1
                link.wait(("y2", q, kind, o, s), slot(kind, q, o, 4 - s, 0))
                piece = slot(kind, q, o, 4 - s, 0, h)
                link.send(("yf", q, kind, 0, o, s), piece, piece, to_y[s])
                link.wait(("x2", q, kind, o, s), slot(kind, q, 4 - s, o, 1))
                piece = slot(kind, q, 4 - s, o, 1, h)
                link.send(("xf", q, kind, 1, o, s), piece, piece, to_x[s])

    def last(q, kind):
        for s in (1, 3):
            h = 0 if s == 1 else 1
            for o in range(4):
                link.wait(("yf", q, kind, 0, o, s), slot(kind, q, o, 2, 0, h))
                link.wait(("xf", q, kind, 1, o, s), slot(kind, q, 2, o, 1, h))

    start(0, "dn")
    loads = []
    for n, (src, dst) in enumerate(((tok_hbm, tok), (cot_hbm, cot), (wdn, slot("dn", 0, 0, 0)))):
        copy = pltpu.make_async_copy(src, dst, local_sem.at[n])
        copy.start()
        loads.append(copy)
    fetch.wait()
    wide[...] = raw[...].astype(F32)
    halves = [wide[:, n, :].astype(BF16) for n in (0, 1)]
    for n in (0, 1):
        flat[:, FF * n:FF * (n + 1)] = halves[n]
    for n in (0, 1):
        fin[zh, x, y, :, FF * n:FF * (n + 1)] = halves[n]
    for kind in ("in", "dn"):
        link.send(("z", kind), own[kind], slot(kind, 0, 0, 0), partner)
    start(0, "in")

    experts = lax.broadcasted_iota(jnp.int32, (8, 128), 0)
    member = jnp.zeros((8, 128), F32)
    coef = jnp.zeros((8, 128), F32)
    for k in range(6):
        hit = jnp.broadcast_to(rt[k:k + 1, :], (8, 128)) == experts
        member = member + jnp.where(hit, 1.0, 0.0)
        coef = coef + jnp.where(hit, jnp.broadcast_to(rw[k:k + 1, :], (8, 128)), 0.0)
    before = lax.broadcasted_iota(jnp.int32, (128, 128), 0) < lax.broadcasted_iota(jnp.int32, (128, 128), 1)
    rank = dot(jnp.where(member > 0.5, 1.0, 0.0).astype(BF16), jnp.where(before, 1.0, 0.0).astype(BF16))
    rank = jnp.where(member > 0.5, rank, -1.0)
    ids = lax.broadcasted_iota(jnp.int32, (CAP, 128), 0).astype(F32)
    for copy in loads[:2]:
        copy.wait()
    tok_v, cot_v = tok[...], cot[...]
    for k in range(8):
        hits = jnp.broadcast_to(rank[k:k + 1, :], (CAP, 128)) == ids
        pick = jnp.where(hits, 1.0, 0.0)
        weight = jnp.where(hits, jnp.broadcast_to(coef[k:k + 1, :], (CAP, 128)), 0.0)
        sx[k] = dot(pick.astype(BF16), tok_v).astype(BF16)
        sdy[k] = (dot(pick.astype(BF16), cot_v) * jnp.sum(weight, axis=1, keepdims=True)).astype(BF16)
        high = weight.astype(BF16)
        back[pl.ds(CAP * k, CAP), :] = pick.astype(BF16)
        whi[pl.ds(CAP * k, CAP), :] = high
        wlo[pl.ds(CAP * k, CAP), :] = (weight - high.astype(F32)).astype(BF16)
    mine = rem(z, 4) * 2 + c
    rx[c] = sx[mine]
    rdy[c] = sdy[mine]

    first(0, "in")
    second(0, "in")
    link.wait(("z", "in"), slot("in", 1, 0, 0))
    start(1, "in")
    rows = []
    for which, (src, dst) in enumerate(((sx, rx), (sdy, rdy))):
        for kind, k, zd in exchange_targets(x, y, z, c):
            if kind == 0:
                if k:
                    continue
                core = 1 - c
            else:
                core = k
            expert = rem(zd, 4) * 2 + core
            copy = pltpu.make_async_remote_copy(
                src_ref=src.at[expert], dst_ref=dst.at[2 * kind + c], send_sem=a_send.at[which * 8 + 2 * kind + k],
                recv_sem=a_recv.at[which * 8 + 2 * kind + c], device_id=device(x, y, zd, core), device_id_type=MESH,
            )
            copy.start()
            rows.append(copy)
    third(0, "in", (1, 3))
    first(1, "in")
    third(0, "in", (2,))
    link.wait(("z", "dn"), slot("dn", 1, 0, 0))
    start(1, "dn")
    second(1, "in")
    first(0, "dn")
    third(1, "in", (1, 3))
    first(1, "dn")
    second(0, "dn")
    third(1, "in", (2,))
    second(1, "dn")

    def rows_here(which, dst):
        for number in range(1, 8):
            s = number if number > 1 else 1 - c
            pltpu.make_async_remote_copy(
                src_ref=dst.at[s], dst_ref=dst.at[s], send_sem=a_send.at[which * 8 + number],
                recv_sem=a_recv.at[which * 8 + s], device_id=place_id(), device_id_type=MESH,
            ).wait_recv()

    def gates(q):
        xs = rows_of(rx, ds(zs[q], 1024))

        @pl.loop(0, 6)
        def _(n):
            cols = ds(n, 256)
            value = dot(xs, fin[zs[q], :, :, :, cols].reshape(1024, 256))
            gu[:, cols] = value if q == 0 else gu[:, cols] + value

    for copy in loads[2:]:
        copy.wait()
    rows_here(0, rx)
    last(0, "in")
    gates(0)
    third(0, "dn", (1, 3))
    third(1, "dn", (1, 3))
    last(1, "in")
    gates(1)
    third(0, "dn", (2,))
    third(1, "dn", (2,))

    @pl.loop(0, 3)
    def _(n):
        cols = ds(n, 256)
        ups = pl.ds(pl.multiple_of(FF + n * 256, 256), 256)
        gate = gu[:, cols]
        hidden = (gate * jax.nn.sigmoid(gate) * gu[:, ups]).astype(BF16)
        hid[:, cols] = hidden
        hidt[cols, :] = hidden.T

    rows_here(1, rdy)

    zr = (1 - zh, zh)
    link2 = Link(send_sem2, recv_sem2, N_SEM_B)
    term = {"in": tin, "dn": tdn}
    buf_a = {"in": a_in, "dn": a_dn}
    buf_b = {"in": b_in, "dn": b_dn}
    buf_c = {"in": c_in, "dn": c_dn}
    buf_d = {"in": d_in, "dn": d_dn}
    buf_e = {"in": e_in, "dn": e_dn}
    to = {0: to_y, 1: to_x}
    offsets = (2, 1, 3, 0)

    def terms(q, kind):
        if kind == "dn":
            left = hidt[ds(zr[q], 384), :]

            @pl.loop(0, 4)
            def _(n):
                cols = ds(n, 512)
                tdn[zr[q], :, :, :, cols] = dot(left, rows_of(rdy, cols)).reshape(4, 4, 24, 512).astype(BF16)
        else:
            @pl.loop(0, 4)
            def _(i):
                left = xt[ds(zr[q] * 4 + i, 256), :]
                for n in range(3):
                    cols = pl.ds(512 * n, 512)
                    tin[zr[q], i, :, :, cols] = dot(left, ggu[:, cols]).astype(BF16).reshape(4, 64, 512)

    def block(kind, q, p, ring, other, h=None):
        xo, yo = (other, ring) if p == 0 else (ring, other)
        return part(kind, term[kind].at[zr[q], rem(x + xo, 4), rem(y + yo, 4)], p, h)

    def add(dst, *srcs):
        total = dst[...].astype(F32)
        for src in srcs:
            total = total + src[...].astype(F32)
        dst[...] = total.astype(BF16)

    def r1(q, kind):
        for o in offsets:
            for p in (0, 1):
                for s, h in ((3, 0), (1, 1)):
                    link2.send(("a", q, kind, p, o, s), block(kind, q, p, 2, o, h),
                               buf_a[kind].at[p, q, o, h], to[p][s])

    def r2(q, kind):
        for o in offsets:
            for p in (0, 1):
                for s, h in ((3, 0), (1, 1)):
                    link2.wait(("a", q, kind, p, o, s), buf_a[kind].at[p, q, o, h])
                    add(block(kind, q, p, s, o, h), buf_a[kind].at[p, q, o, h])
                    link2.send(("b", q, kind, p, o, s), block(kind, q, p, s, o),
                               buf_b[kind].at[p, q, o, h], to[p][s])

    def r3(q, kind):
        for o in offsets:
            for p in (0, 1):
                for s, h in ((3, 0), (1, 1)):
                    link2.wait(("b", q, kind, p, o, s), buf_b[kind].at[p, q, o, h])
                add(block(kind, q, p, 0, o), buf_b[kind].at[p, q, o, 0], buf_b[kind].at[p, q, o, 1])
                if o == 2:
                    for s, h in ((3, 0), (1, 1)):
                        link2.send(("c", q, kind, p, s), block(kind, q, p, 0, 2, h),
                                   buf_c[kind].at[p, q, h], to[1 - p][s])
        for s, h in ((3, 0), (1, 1)):
            for p in (0, 1):
                link2.wait(("c", q, kind, p, s), buf_c[kind].at[p, q, h])
                add(block(kind, q, p, 0, s, h), buf_c[kind].at[p, q, h])
                link2.send(("d", q, kind, p, s), block(kind, q, p, 0, s), buf_d[kind].at[p, q, h], to[1 - p][s])

    def wait_d(q, kind):
        for p in (0, 1):
            for s, h in ((3, 0), (1, 1)):
                link2.wait(("d", q, kind, p, s), buf_d[kind].at[p, q, h])

    def r4(q, kind):
        wait_d(q, kind)
        for p in (0, 1):
            add(block(kind, q, p, 0, 0), buf_d[kind].at[p, q, 0], buf_d[kind].at[p, q, 1])
        link2.send(("e", kind), term[kind].at[zr[0], x, y], buf_e[kind], partner)

    for q in (0, 1):
        terms(q, "dn")
        r1(q, "dn")

    last(0, "dn")
    last(1, "dn")

    @pl.loop(0, 8)
    def _(g):
        for n in range(4):
            cols = pl.ds(512 * n, 512)
            wd[ds(g, 96), cols] = fdn[div(g, 4), rem(g, 4), :, :, cols].astype(F32).reshape(96, 512).astype(BF16)

    r2(0, "dn")
    dy = rows_of(rdy)

    @pl.loop(0, 3)
    def _(n):
        gh[:, ds(n, 256)] = dot(dy, wd[ds(n, 256), :], ((1,), (1,)))

    @pl.loop(0, 3)
    def _(n):
        cols = ds(n, 256)
        ups = pl.ds(pl.multiple_of(FF + n * 256, 256), 256)
        gate, up, grad = gu[:, cols], gu[:, ups], gh[:, cols]
        sig = jax.nn.sigmoid(gate)
        ggu[:, cols] = (grad * up * sig * (1.0 + gate * (1.0 - sig))).astype(BF16)
        ggu[:, ups] = (grad * (gate * sig)).astype(BF16)

    @pl.loop(0, 8)
    def _(n):
        xt[ds(n, 256), :] = rows_of(rx, ds(n, 256)).T

    terms(0, "in")
    r1(0, "in")
    r2(1, "dn")
    terms(1, "in")
    r1(1, "in")

    def rows_back(which, src, dst):
        for number in range(1, 8):
            if number == 1:
                s, zd, core = 1 - c, z, 1 - c
            else:
                off = {2: 7, 3: 7, 4: 1, 5: 1, 6: 6, 7: 2}[number]
                s, zd, core = number, rem(z + off, 8), number % 2
            copy = pltpu.make_async_remote_copy(
                src_ref=src.at[s], dst_ref=dst.at[e], send_sem=r_send.at[which * 8 + number],
                recv_sem=r_recv.at[which * 8 + 2 * (number // 2) + c], device_id=device(x, y, zd, core),
                device_id_type=MESH,
            )
            copy.start()
            rows.append(copy)
        dst[e] = src[c]

    hidden = hid[...]

    @pl.loop(0, 8)
    def _(n):
        cols = ds(n, 256)
        ox[:, :, cols] = dot(hidden, wd[:, cols]).astype(BF16).reshape(8, CAP, 256)

    rows_back(0, ox, box)
    gated = ggu[...]

    @pl.loop(0, 8)
    def _(g):
        value = dot(gated, fin[div(g, 4), rem(g, 4)].reshape(256, 2 * FF), ((1,), (1,)))
        odx[:, :, ds(g, 256)] = value.astype(BF16).reshape(8, CAP, 256)

    rows_back(1, odx, bdx)
    r2(0, "in")
    r3(0, "dn")
    r2(1, "in")
    r4(0, "dn")
    r3(0, "in")
    r3(1, "dn")
    r4(0, "in")
    for which, dst in enumerate((box, bdx)):
        for kind, k, zd in exchange_targets(x, y, z, c):
            if kind == 0:
                if k:
                    continue
                core = 1 - c
            else:
                core = k
            expert = rem(zd, 4) * 2 + core
            pltpu.make_async_remote_copy(
                src_ref=dst.at[expert], dst_ref=dst.at[expert], send_sem=r_send.at[which * 8 + 1],
                recv_sem=r_recv.at[which * 8 + 2 * kind + core], device_id=place_id(), device_id_type=MESH,
            ).wait_recv()
    back_t, high_t, low_t = back[...].T, whi[...].T, wlo[...].T

    @pl.loop(0, 4)
    def _(n):
        cols = ds(n, 512)
        value = rows_of(box, cols)
        layer[:, cols] = (dot(high_t, value) + dot(low_t, value)).astype(BF16)
        gtok[:, cols] = dot(back_t, rows_of(bdx, cols)).astype(BF16)

    outs = []

    def leave(src, dst):
        copy = pltpu.make_async_copy(src, dst, out_sem.at[len(outs)])
        copy.start()
        outs.append(copy)

    leave(layer, layer_hbm)
    leave(gtok, gtok_hbm)
    r3(1, "in")
    for kind in ("dn", "in"):
        wait_d(1, kind)
        link2.wait(("e", kind), buf_e[kind])
        for p in (0, 1):
            total = block(kind, 1, p, 0, 0)[...].astype(F32) + buf_d[kind][p, 1, 0].astype(F32)
            total = total + buf_d[kind][p, 1, 1].astype(F32)
            total = total + part(kind, buf_e[kind], p)[...].astype(F32)
            if kind == "dn":
                part(kind, gdn, p)[...] = total
            else:
                for n in (0, 1):
                    gin[pl.ds(32 * p, 32), n, :] = total[:, FF * n:FF * (n + 1)]
        leave(*((gdn, gdn_hbm) if kind == "dn" else (gin, gin_hbm)))
    for copy in rows:
        copy.wait_send()
    link.drain()
    link2.drain()
    for copy in outs:
        copy.wait()


def deliver(*refs):
    sources, targets, buffers, in_sem, out_sem = refs[:4], refs[4:8], refs[8:12], refs[12], refs[13]
    arrive = [pltpu.make_async_copy(sources[n], buffers[n], in_sem.at[n]) for n in range(4)]
    leave = [pltpu.make_async_copy(buffers[n], targets[n], out_sem.at[n]) for n in range(4)]
    for copy in arrive:
        copy.start()
    for n in range(4):
        arrive[n].wait()
        leave[n].start()
    for copy in leave:
        copy.wait()


RESULTS = (((128, D), BF16), ((128, D), BF16), ((64, 2, FF), F32), ((24, D), F32))


def hand_over(results):
    anyspace = pl.BlockSpec(memory_space=pl.ANY)
    return pl.pallas_call(
        deliver,
        name="deliver",
        out_shape=tuple(jax.ShapeDtypeStruct(shape, kind) for shape, kind in RESULTS),
        in_specs=[anyspace] * 4,
        out_specs=[anyspace] * 4,
        scratch_shapes=[pltpu.VMEM(shape, kind) for shape, kind in RESULTS]
        + [pltpu.SemaphoreType.DMA((4,)), pltpu.SemaphoreType.DMA((4,))],
    )(*results)


def call(tokens, cotangent, routes, weights, win, wdn):
    anyspace = pl.BlockSpec(memory_space=pl.ANY)
    vmem = pl.BlockSpec(memory_space=pltpu.VMEM)
    rows = pltpu.VMEM((8, CAP, D), BF16)
    return pl.pallas_call(
        kernel,
        name="expert_window",
        out_shape=tuple(jax.ShapeDtypeStruct(shape, kind) for shape, kind in RESULTS),
        in_specs=[anyspace, anyspace, vmem, vmem, anyspace, anyspace],
        out_specs=[anyspace] * 4,
        scratch_shapes=[pltpu.VMEM(shape, kind) for shape, kind in RESULTS] + [
            pltpu.VMEM((64, 2, FF), BF16),
            pltpu.VMEM((64, 2 * FF), BF16),
            pltpu.VMEM((64, 2, FF), F32),
            pltpu.VMEM((128, D), BF16),
            pltpu.VMEM((128, D), BF16),
            pltpu.VMEM((2, 4, 4, 64, 2 * FF), BF16),
            pltpu.VMEM((2, 4, 4, 24, D), BF16),
            pltpu.VMEM((FF, D), BF16),
            rows, rows, rows, rows, rows, rows, rows, rows,
            pltpu.VMEM((ROWS, 128), BF16),
            pltpu.VMEM((ROWS, 128), BF16),
            pltpu.VMEM((ROWS, 128), BF16),
            pltpu.VMEM((D, ROWS), BF16),
            pltpu.VMEM((ROWS, 2 * FF), F32),
            pltpu.VMEM((ROWS, FF), F32),
            pltpu.VMEM((ROWS, FF), BF16),
            pltpu.VMEM((FF, ROWS), BF16),
            pltpu.VMEM((ROWS, 2 * FF), BF16),
            pltpu.VMEM((2, 4, 4, 64, 2 * FF), BF16),
            pltpu.VMEM((2, 4, 4, 24, D), BF16),
            pltpu.VMEM((2, 2, 4, 2, 16, 2 * FF), BF16),
            pltpu.VMEM((2, 2, 4, 2, 24, 512), BF16),
            pltpu.VMEM((2, 2, 4, 2, 32, 2 * FF), BF16),
            pltpu.VMEM((2, 2, 4, 2, 24, 1024), BF16),
            pltpu.VMEM((2, 2, 2, 16, 2 * FF), BF16),
            pltpu.VMEM((2, 2, 2, 24, 512), BF16),
            pltpu.VMEM((2, 2, 2, 32, 2 * FF), BF16),
            pltpu.VMEM((2, 2, 2, 24, 1024), BF16),
            pltpu.VMEM((64, 2 * FF), BF16),
            pltpu.VMEM((24, D), BF16),
            pltpu.SemaphoreType.DMA((N_SEM_A,)),
            pltpu.SemaphoreType.DMA((N_SEM_A,)),
            pltpu.SemaphoreType.DMA((16,)),
            pltpu.SemaphoreType.DMA((16,)),
            pltpu.SemaphoreType.DMA((N_SEM_B,)),
            pltpu.SemaphoreType.DMA((N_SEM_B,)),
            pltpu.SemaphoreType.DMA((16,)),
            pltpu.SemaphoreType.DMA((16,)),
            pltpu.SemaphoreType.DMA((4,)),
            pltpu.SemaphoreType.DMA((4,)),
        ],
        compiler_params=pltpu.CompilerParams(
            collective_id=0, has_side_effects=True, vmem_limit_bytes=60 * 1024 * 1024
        ),
    )(tokens, cotangent, routes, weights, win, wdn)


def local(tokens, routes, route_weight, w_in, w_down, cotangent):
    layer_out, grad_tokens, grad_in, grad_down = hand_over(call(
        tokens, cotangent, routes.T, route_weight.T, w_in[0], w_down[0]
    ))
    return layer_out, grad_tokens, grad_in.reshape(w_in.shape), grad_down.reshape(w_down.shape)


def solution(mesh):
    in_specs = (
        P(("fsdp", "ep"), None),
        P(("fsdp", "ep"), None),
        P(("fsdp", "ep"), None),
        P("ep", "fsdp", None, None),
        P("ep", "fsdp", None),
        P(("fsdp", "ep"), None),
    )
    out_specs = (
        P(("fsdp", "ep"), None),
        P(("fsdp", "ep"), None),
        P("ep", "fsdp", None, None),
        P("ep", "fsdp", None),
    )
    return jax.shard_map(local, mesh=mesh, in_specs=in_specs, out_specs=out_specs, check_vma=False)
```

```python
import jax
import jax.numpy as jnp
from jax import lax
from jax.experimental import pallas as pl
from jax.experimental.pallas import tpu as pltpu
from jax.sharding import PartitionSpec as P

D = 2048
FF = 768
CAP = 32
MESH = pl.DeviceIdType.MESH
F32 = jnp.float32
BF16 = jnp.bfloat16
N_SEM_A = 200
N_SEM_B = 220
ROWS = 8 * CAP


def rem(value, modulus):
    return lax.rem(value, jnp.int32(modulus))


def div(value, divisor):
    return lax.div(value, jnp.int32(divisor))


def place():
    f = lax.axis_index("fsdp")
    e = lax.axis_index("ep")
    return rem(div(f, 4), 4), rem(f, 4), div(f, 16) * 4 + div(e, 2), rem(e, 2)


def device(x, y, z, c):
    return (div(z, 4) * 16 + x * 4 + y, rem(z, 4) * 2 + c)


def greet(x, y, z, c):
    barrier = pltpu.get_barrier_semaphore()
    peers = [device(rem(x + o, 4), y, z, c) for o in (1, 3)]
    peers += [device(x, rem(y + o, 4), z, c) for o in (1, 3)]
    peers += [device(x, y, rem(z + 4, 8), c), device(x, y, z, 1 - c)]
    peers += [device(x, y, rem(z + o, 8), k) for o in (1, 7, 2, 6) for k in (0, 1)]
    for peer in peers:
        pl.semaphore_signal(barrier, inc=1, device_id=peer, device_id_type=MESH)
    pl.semaphore_wait(barrier, len(peers))


class Link:
    def __init__(self, send_sem, recv_sem, limit):
        self.send_sem, self.recv_sem, self.limit = send_sem, recv_sem, limit
        self.number, self.sent = {}, []

    def index(self, key):
        number = self.number.setdefault(key, len(self.number))
        assert number < self.limit
        return number

    def send(self, key, src, dst, to):
        k = self.index(key)
        copy = pltpu.make_async_remote_copy(
            src_ref=src, dst_ref=dst, send_sem=self.send_sem.at[k], recv_sem=self.recv_sem.at[k],
            device_id=to, device_id_type=MESH,
        )
        copy.start()
        self.sent.append(copy)

    def wait(self, key, dst):
        k = self.index(key)
        pltpu.make_async_remote_copy(
            src_ref=dst, dst_ref=dst, send_sem=self.send_sem.at[k], recv_sem=self.recv_sem.at[k],
            device_id=place_id(), device_id_type=MESH,
        ).wait_recv()

    def drain(self):
        for copy in self.sent:
            copy.wait_send()


def place_id():
    return (lax.axis_index("fsdp"), lax.axis_index("ep"))


def part(kind, ref, p=None, h=None):
    if p is None:
        return ref
    size = (32 if kind == "in" else 1024) // (1 if h is None else 2)
    start = (32 if kind == "in" else 1024) * p + size * (h or 0)
    if kind == "in":
        return ref.at[pl.ds(start, size), :]
    return ref.at[:, pl.ds(start, size)]


def exchange_targets(x, y, z, c):
    out = []
    for kind, off in ((0, 0), (1, 1), (2, 7), (3, 2 + 4 * c)):
        for k in (0, 1):
            out.append((kind, k, rem(z + off, 8)))
    return out


def dot(left, right, dims=((1,), (0,))):
    return lax.dot_general(left, right, (dims, ((), ())), preferred_element_type=F32)


def ds(index, size):
    return pl.ds(pl.multiple_of(index * size, size), size)


def rows_of(ref, cols=None):
    if cols is None:
        return ref[...].reshape(ROWS, D)
    return ref[:, :, cols].reshape(ROWS, cols.size)


def kernel(tok_hbm, cot_hbm, rt, rw, win, wdn, layer_hbm, gtok_hbm, gin_hbm, gdn_hbm,
           layer, gtok, gin, gdn, raw, flat, wide, tok, cot, fin, fdn, wd, sx, sdy, rx, rdy, ox, odx, box, bdx,
           back, whi, wlo, xt, gu, gh, hid, hidt, ggu,
           tin, tdn, a_in, a_dn, b_in, b_dn, c_in, c_dn, d_in, d_dn, e_in, e_dn,
           send_sem, recv_sem, a_send, a_recv, send_sem2, recv_sem2, r_send, r_recv, local_sem, out_sem):
    x, y, z, c = place()
    zh = div(z, 4)
    e = lax.axis_index("ep")
    fetch = pltpu.make_async_copy(win, raw, local_sem.at[3])
    fetch.start()
    greet(x, y, z, c)
    link = Link(send_sem, recv_sem, N_SEM_A)
    full = {"in": fin, "dn": fdn}
    own = {"in": flat, "dn": wdn}
    zs = (zh, 1 - zh)
    to_x = {s: device(rem(x + s, 4), y, z, c) for s in (1, 3)}
    to_y = {s: device(x, rem(y + s, 4), z, c) for s in (1, 3)}
    partner = device(x, y, rem(z + 4, 8), c)

    def slot(kind, q, xo, yo, p=None, h=None):
        return part(kind, full[kind].at[zs[q], rem(x + xo, 4), rem(y + yo, 4)], p, h)

    def start(q, kind):
        src = own[kind] if q == 0 else slot(kind, q, 0, 0)
        for s in (1, 3):
            link.send(("x0", q, kind, s), src, slot(kind, q, 0, 0), to_x[s])
            link.send(("y0", q, kind, s), src, slot(kind, q, 0, 0), to_y[s])

    def first(q, kind):
        for s in (1, 3):
            h = 0 if s == 1 else 1
            link.wait(("x0", q, kind, s), slot(kind, q, 4 - s, 0))
            for p in (0, 1):
                piece = slot(kind, q, 4 - s, 0, p, h)
                link.send(("xf", q, kind, p, 0, s), piece, piece, to_x[s])
            for t in (1, 3):
                piece = slot(kind, q, 4 - s, 0, 0)
                link.send(("y2", q, kind, 4 - s, t), piece, piece, to_y[t])
            link.wait(("y0", q, kind, s), slot(kind, q, 0, 4 - s))
            for p in (0, 1):
                piece = slot(kind, q, 0, 4 - s, p, h)
                link.send(("yf", q, kind, p, 0, s), piece, piece, to_y[s])
            for t in (1, 3):
                piece = slot(kind, q, 0, 4 - s, 1)
                link.send(("x2", q, kind, 4 - s, t), piece, piece, to_x[t])

    def second(q, kind):
        for s in (1, 3):
            h = 0 if s == 1 else 1
            link.wait(("xf", q, kind, 0, 0, s), slot(kind, q, 2, 0, 0, h))
            link.wait(("yf", q, kind, 1, 0, s), slot(kind, q, 0, 2, 1, h))
        for t in (1, 3):
            piece = slot(kind, q, 2, 0, 0)
            link.send(("y2", q, kind, 2, t), piece, piece, to_y[t])
            piece = slot(kind, q, 0, 2, 1)
            link.send(("x2", q, kind, 2, t), piece, piece, to_x[t])

    def third(q, kind, offsets):
        for o in offsets:
            for s in (1, 3):
                h = 0 if s == 1 else 1
                link.wait(("y2", q, kind, o, s), slot(kind, q, o, 4 - s, 0))
                piece = slot(kind, q, o, 4 - s, 0, h)
                link.send(("yf", q, kind, 0, o, s), piece, piece, to_y[s])
                link.wait(("x2", q, kind, o, s), slot(kind, q, 4 - s, o, 1))
                piece = slot(kind, q, 4 - s, o, 1, h)
                link.send(("xf", q, kind, 1, o, s), piece, piece, to_x[s])

    def last(q, kind):
        for s in (1, 3):
            h = 0 if s == 1 else 1
            for o in range(4):
                link.wait(("yf", q, kind, 0, o, s), slot(kind, q, o, 2, 0, h))
                link.wait(("xf", q, kind, 1, o, s), slot(kind, q, 2, o, 1, h))

    start(0, "dn")
    loads = []
    for n, (src, dst) in enumerate(((tok_hbm, tok), (cot_hbm, cot), (wdn, slot("dn", 0, 0, 0)))):
        copy = pltpu.make_async_copy(src, dst, local_sem.at[n])
        copy.start()
        loads.append(copy)
    fetch.wait()
    wide[...] = raw[...].astype(F32)
    halves = [wide[:, n, :].astype(BF16) for n in (0, 1)]
    for n in (0, 1):
        flat[:, FF * n:FF * (n + 1)] = halves[n]
    for n in (0, 1):
        fin[zh, x, y, :, FF * n:FF * (n + 1)] = halves[n]
    for kind in ("in", "dn"):
        link.send(("z", kind), own[kind], slot(kind, 0, 0, 0), partner)
    start(0, "in")

    experts = lax.broadcasted_iota(jnp.int32, (8, 128), 0)
    member = jnp.zeros((8, 128), F32)
    coef = jnp.zeros((8, 128), F32)
    for k in range(6):
        hit = jnp.broadcast_to(rt[k:k + 1, :], (8, 128)) == experts
        member = member + jnp.where(hit, 1.0, 0.0)
        coef = coef + jnp.where(hit, jnp.broadcast_to(rw[k:k + 1, :], (8, 128)), 0.0)
    before = lax.broadcasted_iota(jnp.int32, (128, 128), 0) < lax.broadcasted_iota(jnp.int32, (128, 128), 1)
    rank = dot(jnp.where(member > 0.5, 1.0, 0.0).astype(BF16), jnp.where(before, 1.0, 0.0).astype(BF16))
    rank = jnp.where(member > 0.5, rank, -1.0)
    ids = lax.broadcasted_iota(jnp.int32, (CAP, 128), 0).astype(F32)
    for copy in loads[:2]:
        copy.wait()
    tok_v, cot_v = tok[...], cot[...]
    for k in range(8):
        hits = jnp.broadcast_to(rank[k:k + 1, :], (CAP, 128)) == ids
        pick = jnp.where(hits, 1.0, 0.0)
        weight = jnp.where(hits, jnp.broadcast_to(coef[k:k + 1, :], (CAP, 128)), 0.0)
        sx[k] = dot(pick.astype(BF16), tok_v).astype(BF16)
        sdy[k] = (dot(pick.astype(BF16), cot_v) * jnp.sum(weight, axis=1, keepdims=True)).astype(BF16)
        high = weight.astype(BF16)
        back[pl.ds(CAP * k, CAP), :] = pick.astype(BF16)
        whi[pl.ds(CAP * k, CAP), :] = high
        wlo[pl.ds(CAP * k, CAP), :] = (weight - high.astype(F32)).astype(BF16)
    mine = rem(z, 4) * 2 + c
    rx[c] = sx[mine]
    rdy[c] = sdy[mine]

    first(0, "dn")
    first(0, "in")
    rows = []
    for which, (src, dst) in enumerate(((sx, rx), (sdy, rdy))):
        for kind, k, zd in exchange_targets(x, y, z, c):
            if kind == 0:
                if k:
                    continue
                core = 1 - c
            else:
                core = k
            expert = rem(zd, 4) * 2 + core
            copy = pltpu.make_async_remote_copy(
                src_ref=src.at[expert], dst_ref=dst.at[2 * kind + c], send_sem=a_send.at[which * 8 + 2 * kind + k],
                recv_sem=a_recv.at[which * 8 + 2 * kind + c], device_id=device(x, y, zd, core), device_id_type=MESH,
            )
            copy.start()
            rows.append(copy)
    second(0, "in")
    third(0, "in", (1, 3))
    link.wait(("z", "in"), slot("in", 1, 0, 0))
    start(1, "in")
    third(0, "in", (2,))
    first(1, "in")
    link.wait(("z", "dn"), slot("dn", 1, 0, 0))
    start(1, "dn")
    second(1, "in")
    third(1, "in", (1, 3))
    first(1, "dn")
    second(0, "dn")
    third(1, "in", (2,))
    second(1, "dn")

    def rows_here(which, dst):
        for number in range(1, 8):
            s = number if number > 1 else 1 - c
            pltpu.make_async_remote_copy(
                src_ref=dst.at[s], dst_ref=dst.at[s], send_sem=a_send.at[which * 8 + number],
                recv_sem=a_recv.at[which * 8 + s], device_id=place_id(), device_id_type=MESH,
            ).wait_recv()

    def gates(q):
        xs = rows_of(rx, ds(zs[q], 1024))

        @pl.loop(0, 6)
        def _(n):
            cols = ds(n, 256)
            value = dot(xs, fin[zs[q], :, :, :, cols].reshape(1024, 256))
            gu[:, cols] = value if q == 0 else gu[:, cols] + value

    for copy in loads[2:]:
        copy.wait()
    rows_here(0, rx)
    last(0, "in")
    gates(0)
    third(0, "dn", (1, 3))
    third(1, "dn", (1, 3))
    last(1, "in")
    gates(1)
    third(0, "dn", (2,))
    third(1, "dn", (2,))

    @pl.loop(0, 3)
    def _(n):
        cols = ds(n, 256)
        ups = pl.ds(pl.multiple_of(FF + n * 256, 256), 256)
        gate = gu[:, cols]
        hidden = (gate * jax.nn.sigmoid(gate) * gu[:, ups]).astype(BF16)
        hid[:, cols] = hidden
        hidt[cols, :] = hidden.T

    rows_here(1, rdy)

    zr = (1 - zh, zh)
    link2 = Link(send_sem2, recv_sem2, N_SEM_B)
    term = {"in": tin, "dn": tdn}
    buf_a = {"in": a_in, "dn": a_dn}
    buf_b = {"in": b_in, "dn": b_dn}
    buf_c = {"in": c_in, "dn": c_dn}
    buf_d = {"in": d_in, "dn": d_dn}
    buf_e = {"in": e_in, "dn": e_dn}
    to = {0: to_y, 1: to_x}
    offsets = (2, 1, 3, 0)

    def terms(q, kind):
        if kind == "dn":
            left = hidt[ds(zr[q], 384), :]

            @pl.loop(0, 4)
            def _(n):
                cols = ds(n, 512)
                tdn[zr[q], :, :, :, cols] = dot(left, rows_of(rdy, cols)).reshape(4, 4, 24, 512).astype(BF16)
        else:
            @pl.loop(0, 4)
            def _(i):
                left = xt[ds(zr[q] * 4 + i, 256), :]
                for n in range(3):
                    cols = pl.ds(512 * n, 512)
                    tin[zr[q], i, :, :, cols] = dot(left, ggu[:, cols]).astype(BF16).reshape(4, 64, 512)

    def block(kind, q, p, ring, other, h=None):
        xo, yo = (other, ring) if p == 0 else (ring, other)
        return part(kind, term[kind].at[zr[q], rem(x + xo, 4), rem(y + yo, 4)], p, h)

    def add(dst, *srcs):
        total = dst[...].astype(F32)
        for src in srcs:
            total = total + src[...].astype(F32)
        dst[...] = total.astype(BF16)

    def r1(q, kind):
        for o in offsets:
            for p in (0, 1):
                for s, h in ((3, 0), (1, 1)):
                    link2.send(("a", q, kind, p, o, s), block(kind, q, p, 2, o, h),
                               buf_a[kind].at[p, q, o, h], to[p][s])

    def r2(q, kind, some=offsets):
        for o in some:
            for p in (0, 1):
                for s, h in ((3, 0), (1, 1)):
                    link2.wait(("a", q, kind, p, o, s), buf_a[kind].at[p, q, o, h])
                    add(block(kind, q, p, s, o, h), buf_a[kind].at[p, q, o, h])
                    link2.send(("b", q, kind, p, o, s), block(kind, q, p, s, o),
                               buf_b[kind].at[p, q, o, h], to[p][s])

    def r3(q, kind):
        for o in offsets:
            for p in (0, 1):
                for s, h in ((3, 0), (1, 1)):
                    link2.wait(("b", q, kind, p, o, s), buf_b[kind].at[p, q, o, h])
                add(block(kind, q, p, 0, o), buf_b[kind].at[p, q, o, 0], buf_b[kind].at[p, q, o, 1])
                if o == 2:
                    for s, h in ((3, 0), (1, 1)):
                        link2.send(("c", q, kind, p, s), block(kind, q, p, 0, 2, h),
                                   buf_c[kind].at[p, q, h], to[1 - p][s])

    def pass_on(q, kind):
        for s, h in ((3, 0), (1, 1)):
            for p in (0, 1):
                link2.wait(("c", q, kind, p, s), buf_c[kind].at[p, q, h])
                add(block(kind, q, p, 0, s, h), buf_c[kind].at[p, q, h])
                link2.send(("d", q, kind, p, s), block(kind, q, p, 0, s), buf_d[kind].at[p, q, h], to[1 - p][s])

    def wait_d(q, kind):
        for p in (0, 1):
            for s, h in ((3, 0), (1, 1)):
                link2.wait(("d", q, kind, p, s), buf_d[kind].at[p, q, h])

    def r4(q, kind):
        wait_d(q, kind)
        for p in (0, 1):
            add(block(kind, q, p, 0, 0), buf_d[kind].at[p, q, 0], buf_d[kind].at[p, q, 1])
        link2.send(("e", kind), term[kind].at[zr[0], x, y], buf_e[kind], partner)

    for q in (0, 1):
        terms(q, "dn")
        r1(q, "dn")

    last(0, "dn")
    last(1, "dn")

    @pl.loop(0, 8)
    def _(g):
        for n in range(4):
            cols = pl.ds(512 * n, 512)
            wd[ds(g, 96), cols] = fdn[div(g, 4), rem(g, 4), :, :, cols].astype(F32).reshape(96, 512).astype(BF16)

    r2(0, "dn")
    dy = rows_of(rdy)

    @pl.loop(0, 3)
    def _(n):
        gh[:, ds(n, 256)] = dot(dy, wd[ds(n, 256), :], ((1,), (1,)))

    @pl.loop(0, 3)
    def _(n):
        cols = ds(n, 256)
        ups = pl.ds(pl.multiple_of(FF + n * 256, 256), 256)
        gate, up, grad = gu[:, cols], gu[:, ups], gh[:, cols]
        sig = jax.nn.sigmoid(gate)
        ggu[:, cols] = (grad * up * sig * (1.0 + gate * (1.0 - sig))).astype(BF16)
        ggu[:, ups] = (grad * (gate * sig)).astype(BF16)

    @pl.loop(0, 8)
    def _(n):
        xt[ds(n, 256), :] = rows_of(rx, ds(n, 256)).T

    terms(0, "in")
    r1(0, "in")
    r2(1, "dn")
    terms(1, "in")
    r1(1, "in")

    def rows_back(which, src, dst):
        for number in range(1, 8):
            if number == 1:
                s, zd, core = 1 - c, z, 1 - c
            else:
                off = {2: 7, 3: 7, 4: 1, 5: 1, 6: 6, 7: 2}[number]
                s, zd, core = number, rem(z + off, 8), number % 2
            copy = pltpu.make_async_remote_copy(
                src_ref=src.at[s], dst_ref=dst.at[e], send_sem=r_send.at[which * 8 + number],
                recv_sem=r_recv.at[which * 8 + 2 * (number // 2) + c], device_id=device(x, y, zd, core),
                device_id_type=MESH,
            )
            copy.start()
            rows.append(copy)
        dst[e] = src[c]

    hidden = hid[...]

    @pl.loop(0, 8)
    def _(n):
        cols = ds(n, 256)
        ox[:, :, cols] = dot(hidden, wd[:, cols]).astype(BF16).reshape(8, CAP, 256)

    rows_back(0, ox, box)
    gated = ggu[...]

    @pl.loop(0, 8)
    def _(g):
        value = dot(gated, fin[div(g, 4), rem(g, 4)].reshape(256, 2 * FF), ((1,), (1,)))
        odx[:, :, ds(g, 256)] = value.astype(BF16).reshape(8, CAP, 256)

    rows_back(1, odx, bdx)
    r2(0, "in")
    r3(0, "dn")
    r2(1, "in", (2,))
    pass_on(0, "dn")
    r3(0, "in")
    r2(1, "in", (1,))
    r4(0, "dn")
    pass_on(0, "in")
    r2(1, "in", (3,))
    r3(1, "dn")
    r2(1, "in", (0,))
    r4(0, "in")
    pass_on(1, "dn")
    for which, dst in enumerate((box, bdx)):
        for kind, k, zd in exchange_targets(x, y, z, c):
            if kind == 0:
                if k:
                    continue
                core = 1 - c
            else:
                core = k
            expert = rem(zd, 4) * 2 + core
            pltpu.make_async_remote_copy(
                src_ref=dst.at[expert], dst_ref=dst.at[expert], send_sem=r_send.at[which * 8 + 1],
                recv_sem=r_recv.at[which * 8 + 2 * kind + core], device_id=place_id(), device_id_type=MESH,
            ).wait_recv()
    back_t, high_t, low_t = back[...].T, whi[...].T, wlo[...].T

    @pl.loop(0, 4)
    def _(n):
        cols = ds(n, 512)
        value = rows_of(box, cols)
        layer[:, cols] = (dot(high_t, value) + dot(low_t, value)).astype(BF16)
        gtok[:, cols] = dot(back_t, rows_of(bdx, cols)).astype(BF16)

    outs = []

    def leave(src, dst):
        copy = pltpu.make_async_copy(src, dst, out_sem.at[len(outs)])
        copy.start()
        outs.append(copy)

    leave(layer, layer_hbm)
    leave(gtok, gtok_hbm)
    r3(1, "in")
    pass_on(1, "in")
    for kind in ("dn", "in"):
        wait_d(1, kind)
        link2.wait(("e", kind), buf_e[kind])
        for p in (0, 1):
            total = block(kind, 1, p, 0, 0)[...].astype(F32) + buf_d[kind][p, 1, 0].astype(F32)
            total = total + buf_d[kind][p, 1, 1].astype(F32)
            total = total + part(kind, buf_e[kind], p)[...].astype(F32)
            if kind == "dn":
                part(kind, gdn, p)[...] = total
            else:
                for n in (0, 1):
                    gin[pl.ds(32 * p, 32), n, :] = total[:, FF * n:FF * (n + 1)]
        leave(*((gdn, gdn_hbm) if kind == "dn" else (gin, gin_hbm)))
    for copy in rows:
        copy.wait_send()
    link.drain()
    link2.drain()
    for copy in outs:
        copy.wait()


def deliver(*refs):
    sources, targets, buffers, in_sem, out_sem = refs[:4], refs[4:8], refs[8:12], refs[12], refs[13]
    arrive = [pltpu.make_async_copy(sources[n], buffers[n], in_sem.at[n]) for n in range(4)]
    leave = [pltpu.make_async_copy(buffers[n], targets[n], out_sem.at[n]) for n in range(4)]
    for copy in arrive:
        copy.start()
    for n in range(4):
        arrive[n].wait()
        leave[n].start()
    for copy in leave:
        copy.wait()


RESULTS = (((128, D), BF16), ((128, D), BF16), ((64, 2, FF), F32), ((24, D), F32))


def hand_over(results):
    anyspace = pl.BlockSpec(memory_space=pl.ANY)
    return pl.pallas_call(
        deliver,
        name="deliver",
        out_shape=tuple(jax.ShapeDtypeStruct(shape, kind) for shape, kind in RESULTS),
        in_specs=[anyspace] * 4,
        out_specs=[anyspace] * 4,
        scratch_shapes=[pltpu.VMEM(shape, kind) for shape, kind in RESULTS]
        + [pltpu.SemaphoreType.DMA((4,)), pltpu.SemaphoreType.DMA((4,))],
    )(*results)


def call(tokens, cotangent, routes, weights, win, wdn):
    anyspace = pl.BlockSpec(memory_space=pl.ANY)
    vmem = pl.BlockSpec(memory_space=pltpu.VMEM)
    rows = pltpu.VMEM((8, CAP, D), BF16)
    return pl.pallas_call(
        kernel,
        name="expert_window",
        out_shape=tuple(jax.ShapeDtypeStruct(shape, kind) for shape, kind in RESULTS),
        in_specs=[anyspace, anyspace, vmem, vmem, anyspace, anyspace],
        out_specs=[anyspace] * 4,
        scratch_shapes=[pltpu.VMEM(shape, kind) for shape, kind in RESULTS] + [
            pltpu.VMEM((64, 2, FF), BF16),
            pltpu.VMEM((64, 2 * FF), BF16),
            pltpu.VMEM((64, 2, FF), F32),
            pltpu.VMEM((128, D), BF16),
            pltpu.VMEM((128, D), BF16),
            pltpu.VMEM((2, 4, 4, 64, 2 * FF), BF16),
            pltpu.VMEM((2, 4, 4, 24, D), BF16),
            pltpu.VMEM((FF, D), BF16),
            rows, rows, rows, rows, rows, rows, rows, rows,
            pltpu.VMEM((ROWS, 128), BF16),
            pltpu.VMEM((ROWS, 128), BF16),
            pltpu.VMEM((ROWS, 128), BF16),
            pltpu.VMEM((D, ROWS), BF16),
            pltpu.VMEM((ROWS, 2 * FF), F32),
            pltpu.VMEM((ROWS, FF), F32),
            pltpu.VMEM((ROWS, FF), BF16),
            pltpu.VMEM((FF, ROWS), BF16),
            pltpu.VMEM((ROWS, 2 * FF), BF16),
            pltpu.VMEM((2, 4, 4, 64, 2 * FF), BF16),
            pltpu.VMEM((2, 4, 4, 24, D), BF16),
            pltpu.VMEM((2, 2, 4, 2, 16, 2 * FF), BF16),
            pltpu.VMEM((2, 2, 4, 2, 24, 512), BF16),
            pltpu.VMEM((2, 2, 4, 2, 32, 2 * FF), BF16),
            pltpu.VMEM((2, 2, 4, 2, 24, 1024), BF16),
            pltpu.VMEM((2, 2, 2, 16, 2 * FF), BF16),
            pltpu.VMEM((2, 2, 2, 24, 512), BF16),
            pltpu.VMEM((2, 2, 2, 32, 2 * FF), BF16),
            pltpu.VMEM((2, 2, 2, 24, 1024), BF16),
            pltpu.VMEM((64, 2 * FF), BF16),
            pltpu.VMEM((24, D), BF16),
            pltpu.SemaphoreType.DMA((N_SEM_A,)),
            pltpu.SemaphoreType.DMA((N_SEM_A,)),
            pltpu.SemaphoreType.DMA((16,)),
            pltpu.SemaphoreType.DMA((16,)),
            pltpu.SemaphoreType.DMA((N_SEM_B,)),
            pltpu.SemaphoreType.DMA((N_SEM_B,)),
            pltpu.SemaphoreType.DMA((16,)),
            pltpu.SemaphoreType.DMA((16,)),
            pltpu.SemaphoreType.DMA((4,)),
            pltpu.SemaphoreType.DMA((4,)),
        ],
        compiler_params=pltpu.CompilerParams(
            collective_id=0, has_side_effects=True, vmem_limit_bytes=60 * 1024 * 1024
        ),
    )(tokens, cotangent, routes, weights, win, wdn)


def local(tokens, routes, route_weight, w_in, w_down, cotangent):
    layer_out, grad_tokens, grad_in, grad_down = hand_over(call(
        tokens, cotangent, routes.T, route_weight.T, w_in[0], w_down[0]
    ))
    return layer_out, grad_tokens, grad_in.reshape(w_in.shape), grad_down.reshape(w_down.shape)


def solution(mesh):
    in_specs = (
        P(("fsdp", "ep"), None),
        P(("fsdp", "ep"), None),
        P(("fsdp", "ep"), None),
        P("ep", "fsdp", None, None),
        P("ep", "fsdp", None),
        P(("fsdp", "ep"), None),
    )
    out_specs = (
        P(("fsdp", "ep"), None),
        P(("fsdp", "ep"), None),
        P("ep", "fsdp", None, None),
        P("ep", "fsdp", None),
    )
    return jax.shard_map(local, mesh=mesh, in_specs=in_specs, out_specs=out_specs, check_vma=False)
```
